512 devices in a mesh: gx: 4 (over x), gy: 8 (over y), goal: 16 (over z, core).
Axes of the slice: x: 4, y: 8, z: 8, core: 2. Of those that a mesh axis runs over, the one named last changes fastest.
Arguments:
- potential: float32 [64, 512, 2048], P('goal', 'gx', 'gy'), as said below
- cost: float32 [512, 2048], P('gx', 'gy'), may hold values from 1 to 3
- obstacle: int32 [512, 2048], P('gx', 'gy'), may hold values 0 or 1
- density: float32 [4, 512, 2048], P(None, 'gx', 'gy'), may hold values from 0.1 to 1
- destinations: int32 [64], P('goal'), may hold values from 0 to 1048575, as said below
- group_ids: int32 [64], P('goal'), may hold values from 0 to 3, as said below
Outputs:
- potential_out: float32 [64, 512, 2048], P('goal', 'gx', 'gy')
- velocity: float32 [4, 2, 512, 2048], P(None, None, 'gx', 'gy')
- density_out: float32 [4, 512, 2048], P(None, 'gx', 'gy')
The draws below stay inside these ranges and needn't reach their ends.
Inputs may be any that keep to these rules, and one draw needn't show every extreme that they name: `potential`: potentials are non-negative. `destinations`: row * 2048 + column of the destination cell. `group_ids`: every group serves at least one destination.
All inputs are finite; a program needn't handle non-finite values. No bound on the sum of `obstacle` on one device may be relied on, other than what follows from the above.
Results may differ from the reference program's by a relative error of at most 0.0003.
Values sent between devices are 32-bit elements; how exact they have to be, the bound alone decides.
A program may use at most 64 MiB of HBM per device.

```python
from functools import reduce
import jax
import jax.numpy as jnp
from jax import lax

GROUPS = 4
SWEEPS = 8
NX = 512
NY = 2048
GOALS = 64


def pick_cells(key):
    return jax.random.randint(jax.random.fold_in(key, 7), (GOALS,), 0, NX * NY).astype(jnp.int32)


def draw_destinations(key, part):
    return pick_cells(key)


def draw_group_ids(key, part):
    order = jax.random.permutation(jax.random.fold_in(key, 3), GOALS).astype(jnp.int32)
    spread = jax.random.randint(jax.random.fold_in(key, 5), (GOALS,), 0, GROUPS).astype(jnp.int32)
    return jnp.where(order < GROUPS, order, spread).astype(jnp.int32)


def draw_potential(key, part):
    target = pick_cells(key)
    target_rows = target // NY
    target_cols = target % NY
    row_index = jnp.arange(NX, dtype=jnp.int32)
    col_index = jnp.arange(NY, dtype=jnp.int32)
    distance = jnp.abs(row_index[None, :, None] - target_rows[:, None, None]) + jnp.abs(col_index[None, None, :] - target_cols[:, None, None])
    distance = distance.astype(jnp.float32)
    noise = jax.random.uniform(jax.random.fold_in(key, 9), (GOALS, NX, NY), jnp.float32, 0.0, 0.02)
    return 2.5 + 0.01 * distance + noise


def with_ends(array, stream_key, least, largest):
    longest = array.shape.index(max(array.shape))
    spots = []
    for shift in (0, 1):
        where = [jax.random.randint(jax.random.fold_in(stream_key, axis), (), 0, length) for axis, length in enumerate(array.shape)]
        where[longest] = (where[longest] + shift) % array.shape[longest]
        spots.append(tuple(where))
    return array.at[spots[0]].set(least).at[spots[1]].set(largest)


def shard_levels(own_key, extent, cuts, low, top_value):
    level = 1.0
    for dim, shards_of in cuts:
        draws = jax.random.uniform(jax.random.fold_in(jax.random.fold_in(own_key, 6), dim), (shards_of,), jnp.float32, low / len(cuts), top_value / len(cuts))
        level = level * jnp.repeat(jnp.exp(draws), extent[dim] // shards_of).reshape((-1,) + (1,) * (len(extent) - 1 - dim))
    return level


def setup_inputs(seed: int = 0) -> dict:
    key_list = jax.random.split(jax.random.key(seed), 7)
    potential = draw_potential(jax.random.fold_in(key_list[6], 71), 0)
    cost = jnp.clip(1.0 + 2.0 * jax.random.uniform(key_list[1], (NX, NY), jnp.float32) ** shard_levels(key_list[1], (NX, NY), ((0, 4), (1, 8)), -0.2, 0.2), 1.0, 3.0)
    obstacle = with_ends((jax.random.randint(key_list[2], (NX, NY), 0, 8) < 1).astype(jnp.int32), jax.random.fold_in(key_list[2], 1), 0, 1)
    density = jnp.clip(0.1 + 0.9 * jax.random.uniform(key_list[3], (GROUPS, NX, NY), jnp.float32) ** shard_levels(key_list[3], (GROUPS, NX, NY), ((1, 4), (2, 8)), -0.2, 0.2), 0.1, 1.0)
    destinations = draw_destinations(jax.random.fold_in(key_list[6], 71), 0)
    group_ids = draw_group_ids(jax.random.fold_in(key_list[6], 71), 0)
    return dict(potential=potential, cost=cost, obstacle=obstacle, density=density, destinations=destinations, group_ids=group_ids)


CELL_SIZE = 0.005
SWEEP_TEMP = 0.002
GOAL_TEMP = 0.01
OBSTACLE_COST = 8.0
COURANT = 0.4
FAR_VALUE = 10000.0
NEG_FILL = -1e+30

def relax_sweep(extended, inside_ext, step_cost, pinned):
    centre = extended[..., 1:-1, 1:-1]
    candidates = [centre]
    pairs = ((extended[..., :-2, 1:-1], inside_ext[:-2, 1:-1]), (extended[..., 2:, 1:-1], inside_ext[2:, 1:-1]), (extended[..., 1:-1, :-2], inside_ext[1:-1, :-2]), (extended[..., 1:-1, 2:], inside_ext[1:-1, 2:]))
    for beside, valid in pairs:
        candidates.append(jnp.where(valid, beside + step_cost, FAR_VALUE))
    lowest = reduce(jnp.minimum, candidates)
    weight_sum = reduce(jnp.add, [jnp.exp((lowest - item) / SWEEP_TEMP) for item in candidates])
    return jnp.where(pinned, 0.0, lowest - SWEEP_TEMP * jnp.log(weight_sum))

def advect_step(field_two, density_one, inside_two):
    centre = field_two[:, 1:-1, 1:-1]
    north_value = jnp.where(inside_two[:-2, 1:-1], field_two[:, :-2, 1:-1], centre)
    south_value = jnp.where(inside_two[2:, 1:-1], field_two[:, 2:, 1:-1], centre)
    west_value = jnp.where(inside_two[1:-1, :-2], field_two[:, 1:-1, :-2], centre)
    east_value = jnp.where(inside_two[1:-1, 2:], field_two[:, 1:-1, 2:], centre)
    grad_x = (south_value - north_value) / (2.0 * CELL_SIZE)
    grad_y = (east_value - west_value) / (2.0 * CELL_SIZE)
    speed_factor = 1.0 / (1.0 + lax.optimization_barrier(jnp.sum(density_one, axis=0)))
    scale_factor = speed_factor / jnp.sqrt(1.0 + grad_x * grad_x + grad_y * grad_y)
    flow_x = -scale_factor * grad_x
    flow_y = -scale_factor * grad_y
    inside_one = inside_two[1:-1, 1:-1]
    face_x = 0.5 * (flow_x[:, :-1, 1:-1] + flow_x[:, 1:, 1:-1])
    flux_x = jnp.maximum(face_x, 0.0) * density_one[:, :-1, 1:-1] + jnp.minimum(face_x, 0.0) * density_one[:, 1:, 1:-1]
    flux_x = jnp.where(inside_one[:-1, 1:-1] & inside_one[1:, 1:-1], flux_x, 0.0)
    face_y = 0.5 * (flow_y[:, 1:-1, :-1] + flow_y[:, 1:-1, 1:])
    flux_y = jnp.maximum(face_y, 0.0) * density_one[:, 1:-1, :-1] + jnp.minimum(face_y, 0.0) * density_one[:, 1:-1, 1:]
    flux_y = jnp.where(inside_one[1:-1, :-1] & inside_one[1:-1, 1:], flux_y, 0.0)
    updated = density_one[:, 1:-1, 1:-1] - COURANT * (flux_x[:, 1:] - flux_x[:, :-1] + flux_y[:, :, 1:] - flux_y[:, :, :-1])
    velocity = jnp.stack((flow_x[:, 1:-1, 1:-1], flow_y[:, 1:-1, 1:-1]), axis=1)
    return (velocity, updated)

def reference(potential, cost, obstacle, density, destinations, group_ids):
    step_cost = (cost + OBSTACLE_COST * obstacle.astype(jnp.float32)) * CELL_SIZE
    inside = jnp.ones((NX, NY), dtype=bool)
    inside_pad = jnp.pad(inside, 1)
    row_index = jnp.arange(NX, dtype=jnp.int32)[:, None]
    col_index = jnp.arange(NY, dtype=jnp.int32)[None, :]
    group_index = jnp.arange(GROUPS, dtype=jnp.int32)[:, None, None]

    def per_goal(carry, items):
        field_now, target, group = items
        pinned = (row_index == target // NY) & (col_index == target % NY)
        for sweep_index in range(SWEEPS):
            field_now = relax_sweep(jnp.pad(field_now, 1), inside_pad, step_cost, pinned)
        peak_score, weight_sum = carry
        scores = -field_now / GOAL_TEMP
        member = group_index == group
        new_peak = jnp.where(member, jnp.maximum(peak_score, scores[None]), peak_score)
        weight_sum = jnp.where(member, weight_sum * jnp.exp(peak_score - new_peak) + jnp.exp(scores[None] - new_peak), weight_sum)
        return ((new_peak, weight_sum), field_now)
    start = (jnp.full((GROUPS, NX, NY), NEG_FILL, jnp.float32), jnp.zeros((GROUPS, NX, NY), jnp.float32))
    (peak_score, weight_sum), potential_out = lax.scan(per_goal, start, (potential, destinations, group_ids))
    group_field = -GOAL_TEMP * (peak_score + jnp.log(weight_sum))
    velocity, density_out = advect_step(jnp.pad(group_field, ((0, 0), (2, 2), (2, 2))), jnp.pad(density, ((0, 0), (1, 1), (1, 1))), jnp.pad(inside, 2))
    return (potential_out, velocity, density_out)
```

```python
import functools

import jax
import jax.numpy as jnp
import numpy as np
from jax import lax
from jax.experimental import pallas as pl
from jax.experimental.pallas import tpu as pltpu
from jax.sharding import PartitionSpec as P

MESH = pl.DeviceIdType.MESH
SWEEPS = 8
CELL_SIZE = 0.005
SWEEP_TEMP = 0.002
GOAL_TEMP = 0.01
OBSTACLE_COST = 8.0
COURANT = 0.4
FAR = 10000.0
SHUT = 1e30
ABSENT = 1e28

LANES = 128
PAD = 16
K_SWEEP = float(1.0 / (SWEEP_TEMP * np.log(2.0)))
K_GOAL = float(1.0 / (GOAL_TEMP * np.log(2.0)))


def roll(x, shift):
    shift %= LANES
    return x if shift == 0 else pltpu.roll(x, shift, 1)


def soft_min(items, k, temp):
    least = functools.reduce(jnp.minimum, items)
    total = functools.reduce(jnp.add, [jnp.exp2((least - item) * k) for item in items])
    return least - temp * jnp.log(total)


def loop(start, stop, body, unroll=1):
    def step(i, carry):
        body(i)
        return carry

    lax.fori_loop(start, stop, step, 0, unroll=unroll)


def tile_at(row):
    return pl.ds(pl.multiple_of(row, 8), 8)


def kernel(
    nx, ny, nz, goals, groups, height, width,
    pot, cost, obst, dens, dest, gid,
    pot_out, vel_out, den_out,
    X, St, S, Ss, Cb, Ob, D, Ds, ML, MR, RL, RR,
    G, G2, H, R, F, Fs, FML, FMR, FRL, FRR, Vx, Vy, Vxs, Vys, DO,
    lsem, ssem, rsem,
):
    halves = width // LANES
    rows_all = height + 2 * PAD
    bottom = PAD + height
    chunk = height // nz
    ix, iy, ig = lax.axis_index("gx"), lax.axis_index("gy"), lax.axis_index("goal")
    z, core = ig // 2, ig % 2
    xs = {-1: lax.rem(ix + nx - 1, nx), 0: ix, 1: lax.rem(ix + 1, nx)}
    ys = {-1: lax.rem(iy + ny - 1, ny), 0: iy, 1: lax.rem(iy + 1, ny)}
    partner = (ix, iy, 2 * z + (1 - core))
    z_at = [lax.rem(z + d, nz) for d in range(nz)]
    z_back = [lax.rem(z + nz - d, nz) for d in range(nz)]
    z_peer = [(ix, iy, 2 * z_at[d] + core) for d in range(nz)]
    around = [(dx, dy) for dx in (-1, 0, 1) for dy in (-1, 0, 1) if (dx, dy) != (0, 0)]
    at_top, at_bottom = ix == 0, ix == nx - 1
    at_left, at_right = iy == 0, iy == ny - 1

    barrier = pltpu.get_barrier_semaphore()
    greet = [(xs[dx], ys[dy], ig) for dx, dy in around] + [partner] + z_peer[1:]
    for device in greet:
        pl.semaphore_signal(barrier, inc=1, device_id=device, device_id_type=MESH)

    count = [0]

    def local(src, dst):
        copy = pltpu.make_async_copy(src, dst, lsem.at[count[0]])
        count[0] += 1
        copy.start()
        return copy

    body_rows = pl.ds(PAD, height)
    first, last = pl.ds(0, 8), pl.ds(height - 8, 8)
    above, below = pl.ds(PAD - 8, 8), pl.ds(bottom, 8)
    p_first, p_last = pl.ds(PAD, 8), pl.ds(bottom - 8, 8)
    cut = [pl.ds(LANES * h, LANES) for h in range(halves)]

    cost_in = [local(cost.at[:, cut[h]], Cb.at[h]) for h in range(halves)]
    cost_in += [local(obst.at[:, cut[h]], Ob.at[h]) for h in range(halves)]
    field_in = [local(pot.at[:, :, cut[h]], X.at[0, :, h, body_rows]) for h in range(halves)]
    field_in += [local(dens.at[:, :, cut[h]], D.at[:, h, body_rows]) for h in range(halves)]

    sent = [0]

    def remote(src, dst, device):
        copy = pltpu.make_async_remote_copy(
            src_ref=src, dst_ref=dst, send_sem=ssem.at[sent[0]], recv_sem=rsem.at[sent[0]],
            device_id=device, device_id_type=MESH,
        )
        sent[0] += 1
        copy.start()
        return copy

    pl.semaphore_wait(barrier, len(greet))
    north, south = (xs[-1], ys[0], ig), (xs[1], ys[0], ig)
    halo = []
    for h in range(halves):
        halo.append(remote(pot.at[:, first, cut[h]], X.at[0, :, h, below], north))
        halo.append(remote(pot.at[:, last, cut[h]], X.at[0, :, h, above], south))
        halo.append(remote(dens.at[:, first, cut[h]], D.at[:, h, below], north))
        halo.append(remote(dens.at[:, last, cut[h]], D.at[:, h, above], south))

    lane = lax.broadcasted_iota(jnp.int32, (8, LANES), 1)
    sub = lax.broadcasted_iota(jnp.int32, (8, LANES), 0)
    slot = lane // 32
    offset = lane % 32

    for buffer in (0, 1):
        for h in range(halves):
            for g in range(goals):
                X[buffer, g, h, 0:8] = jnp.zeros((8, LANES), jnp.float32)
                X[buffer, g, h, rows_all - 8 : rows_all] = jnp.zeros((8, LANES), jnp.float32)
            St[buffer, h, 0:8] = jnp.zeros((8, LANES), jnp.float32)
            St[buffer, h, rows_all - 8 : rows_all] = jnp.zeros((8, LANES), jnp.float32)

    for copy in cost_in:
        copy.wait()

    def make_cost(i):
        for h in range(halves):
            blocked = Ob[h, tile_at(8 * i)].astype(jnp.float32)
            S[h, tile_at(PAD + 8 * i)] = (Cb[h, tile_at(8 * i)] + OBSTACLE_COST * blocked) * CELL_SIZE

    loop(0, height // 8, make_cost, unroll=2)
    halo.append(remote(S.at[:, p_first], S.at[:, below], north))
    halo.append(remote(S.at[:, p_last], S.at[:, above], south))
    for copy in field_in:
        copy.wait()

    def in_slots(tiles, shift):
        out = roll(tiles[0], shift)
        for g in range(1, len(tiles)):
            out = jnp.where(slot == g, roll(tiles[g], shift + 32 * g), out)
        return out

    def repeated(tile, shift):
        out = jnp.where(offset < 8, roll(tile, shift), 0.0)
        return out

    right_edge = 8 - LANES

    def pack(i):
        t = tile_at(PAD + 8 * i)
        tm = tile_at(8 * i)
        p = [X[0, g, halves - 1, t] for g in range(goals)]
        s = [S[halves - 1, t]] * goals
        d = [D[k, halves - 1, t] for k in range(groups)]
        out = in_slots(p, right_edge)
        out = jnp.where(offset < 8, out, in_slots(s, right_edge + 8))
        MR[tm] = jnp.where(offset < 16, out, in_slots(d, right_edge + 16))
        p = [X[0, g, 0, t] for g in range(goals)]
        s = [S[0, t]] * goals
        d = [D[k, 0, t] for k in range(groups)]
        out = in_slots(p, 24)
        out = jnp.where(offset >= 24, out, in_slots(s, 16))
        ML[tm] = jnp.where(offset >= 16, out, in_slots(d, 8))

    loop(0, height // 8, pack, unroll=2)

    def send_columns(mr, ml, rl, rr):
        out = [
            remote(mr, rl.at[body_rows], (xs[0], ys[1], ig)),
            remote(ml, rr.at[body_rows], (xs[0], ys[-1], ig)),
            remote(mr.at[first], rl.at[below], (xs[-1], ys[1], ig)),
            remote(mr.at[last], rl.at[above], (xs[1], ys[1], ig)),
            remote(ml.at[first], rr.at[below], (xs[-1], ys[-1], ig)),
            remote(ml.at[last], rr.at[above], (xs[1], ys[-1], ig)),
        ]
        return out

    halo += send_columns(MR, ML, RL, RR)
    for copy in halo:
        copy.wait()

    n_ext = height // 8 + 2
    own_left, own_right = offset >= 8, offset < 24

    def build(i):
        t = tile_at(PAD - 8 + 8 * i)
        from_left, from_right = RL[t], RR[t]
        s = jnp.where(own_left, in_slots([S[0, t]] * goals, 8), roll(from_left, -8))
        s_left = jnp.where(at_left & ~own_left, SHUT, s)
        p = jnp.where(own_left, in_slots([X[0, g, 0, t] for g in range(goals)], 8), from_left)
        St[0, 0, t] = jnp.where(at_left & ~own_left, FAR - roll(s, -1), p)
        Ss[0, t] = s_left
        Ds[0, t] = jnp.where(
            own_left, in_slots([D[k, 0, t] for k in range(groups)], 8), roll(from_left, -16)
        )
        shift = 24 - LANES
        s = jnp.where(own_right, in_slots([S[halves - 1, t]] * goals, shift), roll(from_right, 8))
        s_right = jnp.where(at_right & ~own_right, SHUT, s)
        p = jnp.where(
            own_right, in_slots([X[0, g, halves - 1, t] for g in range(goals)], shift), from_right
        )
        St[0, 1, t] = jnp.where(at_right & ~own_right, FAR - roll(s, 1), p)
        Ss[1, t] = s_right
        Ds[1, t] = jnp.where(
            own_right, in_slots([D[k, halves - 1, t] for k in range(groups)], shift), roll(from_right, 16)
        )

    loop(0, n_ext, build)

    for flag, ghost, inner in ((at_top, above, PAD), (at_bottom, below, bottom - 1)):
        for h in range(halves):
            beside = jnp.broadcast_to(FAR - S[h, inner : inner + 1], (8, LANES))
            for g in range(goals):
                X[0, g, h, ghost] = jnp.where(flag, beside, X[0, g, h, ghost])
            S[h, ghost] = jnp.where(flag, SHUT, S[h, ghost])
        for side in (0, 1):
            beside = Ss[side, inner : inner + 1]
            beside = jnp.where(beside < SHUT, FAR - beside, FAR)
            beside = jnp.broadcast_to(beside, (8, LANES))
            St[0, side, ghost] = jnp.where(flag, beside, St[0, side, ghost])
            Ss[side, ghost] = jnp.where(flag, SHUT, Ss[side, ghost])

    width_all = width * ny
    cell = sub * width + lane
    target, strip_row = [], [jnp.full((8, LANES), -1000, jnp.int32) for _ in (0, 1)]
    for g in range(goals):
        row = dest[g] // width_all - ix * height
        col = dest[g] % width_all - iy * width
        held = (col >= 0) & (col < width)
        target.append(jnp.where(held, row * width + col, -(1 << 24)))
        for side, start in ((0, -8), (1, width - 24)):
            here = (slot == g) & (offset + start == col)
            strip_row[side] = jnp.where(here, row, strip_row[side])

    def relax(centre, up, down, left, right, s):
        return soft_min([centre, up + s, down + s, left + s, right + s], K_SWEEP, SWEEP_TEMP)

    def sweep(now, later, lo, hi):
        def tile(i):
            base = PAD - 8 + 8 * i
            t, tu, td = tile_at(base), pl.ds(base - 1, 8), pl.ds(base + 1, 8)
            row = 8 * i - 8
            s = [S[h, t] for h in range(halves)]
            for g in range(goals):
                centre = [X[now, g, h, t] for h in range(halves)]
                to_right = [roll(c, 1) for c in centre]
                to_left = [roll(c, -1) for c in centre]
                for h in range(halves):
                    left, right = to_right[h], to_left[h]
                    if h > 0:
                        left = jnp.where(lane == 0, to_right[h - 1], left)
                    if h < halves - 1:
                        right = jnp.where(lane == LANES - 1, to_left[h + 1], right)
                    new = relax(centre[h], X[now, g, h, tu], X[now, g, h, td], left, right, s[h])
                    pinned = cell == target[g] - (row * width + LANES * h)
                    X[later, g, h, t] = jnp.where(pinned, 0.0, new)
            for side in (0, 1):
                c = St[now, side, t]
                new = relax(c, St[now, side, tu], St[now, side, td], roll(c, 1), roll(c, -1), Ss[side, t])
                St[later, side, t] = jnp.where(strip_row[side] == sub + row, 0.0, new)

        loop(lo, hi, tile)

    def two_sweeps(j):
        sweep(0, 1, 0, n_ext)
        sweep(1, 0, 0, n_ext)

    loop(0, SWEEPS // 2, two_sweeps)

    bias = [[jnp.where(gid[g] == k, 0.0, ABSENT) for k in range(groups)] for g in range(goals)]

    def merged(main, left, right, g, h):
        if h == 0:
            main = jnp.where(lane < 8, roll(left, -(32 * g + 8)), main)
        if h == halves - 1:
            main = jnp.where(lane >= LANES - 8, roll(right, LANES - 24 - 32 * g), main)
        return main

    def finish(i):
        t = tile_at(PAD + 8 * i)
        strips = [St[0, side, t] for side in (0, 1)]
        for h in range(halves):
            p = [merged(X[0, g, h, t], strips[0], strips[1], g, h) for g in range(goals)]
            for g in range(goals):
                X[0, g, h, t] = p[g]
            for k in range(groups):
                G[k, h, tile_at(8 * i)] = soft_min(
                    [p[g] + bias[g][k] for g in range(goals)], K_GOAL, GOAL_TEMP
                )

    loop(0, height // 8, finish)
    outs = [local(X.at[0, :, h, body_rows], pot_out.at[:, :, cut[h]]) for h in range(halves)]

    swap = remote(G.at[:, 1 - core], G2, partner)
    swap.wait()

    def join(i):
        t = tile_at(8 * i)
        for k in range(groups):
            H[k, t] = soft_min([G[k, core, t], G2[k, t]], K_GOAL, GOAL_TEMP)

    loop(0, height // 8, join)

    def block(j):
        return pl.ds(pl.multiple_of(chunk * j, 8), chunk)

    def field_block(j):
        return pl.ds(pl.multiple_of(PAD + chunk * j, 8), chunk)

    order = sorted(range(1, nz), key=lambda d: -min(d, nz - d))
    spread = [remote(H.at[:, block(z_at[d])], R.at[d], z_peer[d]) for d in order]
    for copy in spread:
        copy.wait()
    for k in range(groups):
        for i in range(chunk // 8):
            t = slice(8 * i, 8 * i + 8)
            items = [H[k, tile_at(chunk * z + 8 * i)]] + [R[d, k, t] for d in range(1, nz)]
            F[k, core, tile_at(PAD + chunk * z + 8 * i)] = soft_min(items, K_GOAL, GOAL_TEMP)

    def mine(j):
        return F.at[:, core, field_block(j)]

    gather = {d: remote(mine(z), mine(z), z_peer[d]) for d in order}
    forward = [remote(mine(z), mine(z), partner)]
    for d in sorted(range(1, nz), key=lambda d: min(d, nz - d)):
        gather[d].wait_recv()
        forward.append(remote(mine(z_back[d]), mine(z_back[d]), partner))
    for d in order:
        gather[d].wait_send()
    for copy in forward:
        copy.wait()

    halo = [
        remote(F.at[:, :, p_first], F.at[:, :, below], north),
        remote(F.at[:, :, p_last], F.at[:, :, above], south),
    ]

    def pack_field(i):
        t = tile_at(PAD + 8 * i)
        FMR[tile_at(8 * i)] = in_slots([F[k, halves - 1, t] for k in range(groups)], right_edge)
        FML[tile_at(8 * i)] = in_slots([F[k, 0, t] for k in range(groups)], 24)

    loop(0, height // 8, pack_field, unroll=2)
    halo += send_columns(FMR, FML, FRL, FRR)
    for copy in halo:
        copy.wait()

    for flag, ghost, inner in ((at_top, above, PAD), (at_bottom, below, bottom - 1)):
        for h in range(halves):
            for k in range(groups):
                beside = jnp.broadcast_to(F[k, h, inner : inner + 1], (8, LANES))
                F[k, h, ghost] = jnp.where(flag, beside, F[k, h, ghost])

    def build_field(i):
        t = tile_at(PAD - 8 + 8 * i)
        f = jnp.where(own_left, in_slots([F[k, 0, t] for k in range(groups)], 8), FRL[t])
        Fs[0, t] = jnp.where(at_left & ~own_left, roll(f, -1), f)
        f = jnp.where(
            own_right, in_slots([F[k, halves - 1, t] for k in range(groups)], 24 - LANES), FRR[t]
        )
        Fs[1, t] = jnp.where(at_right & ~own_right, roll(f, 1), f)

    loop(0, n_ext, build_field)
    for flag, ghost, inner in ((at_top, above, PAD), (at_bottom, below, bottom - 1)):
        for side in (0, 1):
            beside = jnp.broadcast_to(Fs[side, inner : inner + 1], (8, LANES))
            Fs[side, ghost] = jnp.where(flag, beside, Fs[side, ghost])

    inv_two_cells = 1.0 / (2.0 * CELL_SIZE)

    def flow(up, down, left, right, speed):
        gx = (down - up) * inv_two_cells
        gy = (right - left) * inv_two_cells
        scale = speed * lax.rsqrt(1.0 + gx * gx + gy * gy)
        return -scale * gx, -scale * gy

    def sides(tiles, h):
        left, right = roll(tiles[h], 1), roll(tiles[h], -1)
        if h > 0:
            left = jnp.where(lane == 0, roll(tiles[h - 1], 1), left)
        if h < halves - 1:
            right = jnp.where(lane == LANES - 1, roll(tiles[h + 1], -1), right)
        return left, right

    def flows(i):
        base = PAD - 8 + 8 * i
        t, tu, td = tile_at(base), pl.ds(base - 1, 8), pl.ds(base + 1, 8)
        speed = []
        for h in range(halves):
            total = functools.reduce(jnp.add, [D[k, h, t] for k in range(groups)])
            speed.append(1.0 / (1.0 + total))
        for k in range(groups):
            centre = [F[k, h, t] for h in range(halves)]
            for h in range(halves):
                left, right = sides(centre, h)
                Vx[k, h, t], Vy[k, h, t] = flow(F[k, h, tu], F[k, h, td], left, right, speed[h])
        for side in (0, 1):
            d = Ds[side, t]
            d = d + roll(d, 32)
            d = d + roll(d, 64)
            c = Fs[side, t]
            Vxs[side, t], Vys[side, t] = flow(
                Fs[side, tu], Fs[side, td], roll(c, 1), roll(c, -1), 1.0 / (1.0 + d)
            )

    loop(0, n_ext, flows)

    def flux(low_v, high_v, low_d, high_d):
        face = 0.5 * (low_v + high_v)
        return jnp.maximum(face, 0.0) * low_d + jnp.minimum(face, 0.0) * high_d

    def advect(i):
        base = PAD + 8 * i
        t, tu, td = tile_at(base), pl.ds(base - 1, 8), pl.ds(base + 1, 8)
        row = sub + 8 * i
        no_up = at_top & (row == 0)
        no_down = at_bottom & (row == height - 1)

        def updated(vx, vxu, vxd, vy, vyl, vyr, d, du, dd, dl, dr, no_left, no_right):
            up = jnp.where(no_up, 0.0, flux(vxu, vx, du, d))
            down = jnp.where(no_down, 0.0, flux(vx, vxd, d, dd))
            left, right = flux(vyl, vy, dl, d), flux(vy, vyr, d, dr)
            left = left if no_left is None else jnp.where(no_left, 0.0, left)
            right = right if no_right is None else jnp.where(no_right, 0.0, right)
            return d - COURANT * (down - up + right - left)

        strips = []
        for side in (0, 1):
            vy, d = Vys[side, t], Ds[side, t]
            new = updated(
                Vxs[side, t], Vxs[side, tu], Vxs[side, td], vy, roll(vy, 1), roll(vy, -1),
                d, Ds[side, tu], Ds[side, td], roll(d, 1), roll(d, -1),
                (at_left & (offset == 8)) if side == 0 else None,
                (at_right & (offset == 23)) if side == 1 else None,
            )
            strips.append((Vxs[side, t], vy, new))
        for k in range(groups):
            vy = [Vy[k, h, t] for h in range(halves)]
            d = [D[k, h, t] for h in range(halves)]
            fresh = []
            for h in range(halves):
                vyl, vyr = sides(vy, h)
                dl, dr = sides(d, h)
                new = updated(
                    Vx[k, h, t], Vx[k, h, tu], Vx[k, h, td], vy[h], vyl, vyr,
                    d[h], D[k, h, tu], D[k, h, td], dl, dr, None, None,
                )
                fresh.append(new)
            for h in range(halves):
                DO[k, h, tile_at(8 * i)] = merged(fresh[h], strips[0][2], strips[1][2], k, h)

    loop(0, height // 8, advect)

    def merge_flow(i):
        t = tile_at(PAD + 8 * i)
        for k in range(groups):
            for h in range(halves):
                Vx[k, h, t] = merged(Vx[k, h, t], Vxs[0, t], Vxs[1, t], k, h)
                Vy[k, h, t] = merged(Vy[k, h, t], Vys[0, t], Vys[1, t], k, h)

    loop(0, height // 8, merge_flow)
    for h in range(halves):
        outs.append(local(Vx.at[:, h, body_rows], vel_out.at[:, 0, :, cut[h]]))
        outs.append(local(Vy.at[:, h, body_rows], vel_out.at[:, 1, :, cut[h]]))
        outs.append(local(DO.at[:, h], den_out.at[:, :, cut[h]]))
    for copy in outs:
        copy.wait()


def solution(mesh):
    nx, ny, ng = mesh.shape["gx"], mesh.shape["gy"], mesh.shape["goal"]

    def per_device(potential, cost, obstacle, density, destinations, group_ids):
        goals, height, width = potential.shape
        groups = density.shape[0]
        halves = width // LANES
        rows = height + 2 * PAD
        nz = ng // 2
        f32 = jnp.float32

        def vm(*shape, dtype=f32):
            return pltpu.VMEM(shape, dtype)

        panel = (rows, LANES)
        flat = (height, LANES)
        scratch = [
            vm(2, goals, halves, *panel), vm(2, 2, *panel), vm(halves, *panel), vm(2, *panel),
            vm(halves, *flat), vm(halves, *flat, dtype=jnp.int32),
            vm(groups, halves, *panel), vm(2, *panel), vm(*flat), vm(*flat), vm(*panel), vm(*panel),
            vm(groups, halves, *flat), vm(groups, *flat), vm(groups, *flat),
            vm(nz, groups, height // nz, LANES), vm(groups, halves, *panel), vm(2, *panel),
            vm(*flat), vm(*flat), vm(*panel), vm(*panel),
            vm(groups, halves, *panel), vm(groups, halves, *panel), vm(2, *panel), vm(2, *panel),
            vm(groups, halves, *flat),
            pltpu.SemaphoreType.DMA((24,)),
            pltpu.SemaphoreType.DMA((64,)),
            pltpu.SemaphoreType.DMA((64,)),
        ]
        anywhere = pl.BlockSpec(memory_space=pl.ANY)
        scalars = pl.BlockSpec(memory_space=pltpu.SMEM)
        return pl.pallas_call(
            functools.partial(kernel, nx, ny, nz, goals, groups, height, width),
            out_shape=(
                jax.ShapeDtypeStruct(potential.shape, f32),
                jax.ShapeDtypeStruct((groups, 2, height, width), f32),
                jax.ShapeDtypeStruct(density.shape, f32),
            ),
            in_specs=[anywhere] * 4 + [scalars] * 2,
            out_specs=(anywhere,) * 3,
            scratch_shapes=scratch,
            compiler_params=pltpu.CompilerParams(
                collective_id=0, has_side_effects=True, vmem_limit_bytes=40 << 20
            ),
            name="crowd_step",
        )(potential, cost, obstacle, density, destinations, group_ids)

    in_specs = (
        P("goal", "gx", "gy"),
        P("gx", "gy"),
        P("gx", "gy"),
        P(None, "gx", "gy"),
        P("goal"),
        P("goal"),
    )
    out_specs = (P("goal", "gx", "gy"), P(None, None, "gx", "gy"), P(None, "gx", "gy"))
    return jax.shard_map(
        per_device, mesh=mesh, in_specs=in_specs, out_specs=out_specs, check_vma=False
    )
```

```python
import functools

import jax
import jax.numpy as jnp
import numpy as np
from jax import lax
from jax.experimental import pallas as pl
from jax.experimental.pallas import tpu as pltpu
from jax.sharding import PartitionSpec as P

MESH = pl.DeviceIdType.MESH
SWEEPS = 8
CELL_SIZE = 0.005
SWEEP_TEMP = 0.002
GOAL_TEMP = 0.01
OBSTACLE_COST = 8.0
COURANT = 0.4
FAR = 10000.0
SHUT = 1e30
ABSENT = 1e28

LANES = 128
PAD = 16
U_SWEEP, U_BUILD, U_FIN = 9, 3, 4
K_SWEEP = float(1.0 / (SWEEP_TEMP * np.log(2.0)))
K_GOAL = float(1.0 / (GOAL_TEMP * np.log(2.0)))


def roll(x, shift):
    shift %= LANES
    return x if shift == 0 else pltpu.roll(x, shift, 1)


def soft_min(items, k, temp):
    least = functools.reduce(jnp.minimum, items)
    total = functools.reduce(jnp.add, [jnp.exp2((least - item) * k) for item in items])
    return least - temp * jnp.log(total)


def loop(start, stop, body, unroll=1):
    def step(i, carry):
        body(i)
        return carry

    lax.fori_loop(start, stop, step, 0, unroll=unroll)


def tile_at(row):
    return pl.ds(pl.multiple_of(row, 8), 8)


def kernel(
    nx, ny, nz, goals, groups, height, width,
    pot, cost, obst, dens, dest, gid,
    pot_out, vel_out, den_out,
    XA, XB, SA, SB, S, Ss, Cb, Ob, D, Ds, ML, MR, RL, RR,
    G, G2, H, R, F, Fs, FML, FMR, FRL, FRR, Vx, Vy, Vxs, Vys, DO,
    lsem, ssem, rsem,
):
    X, St = (XA, XB), (SA, SB)
    halves = width // LANES
    rows_all = height + 2 * PAD
    bottom = PAD + height
    ix, iy, ig = lax.axis_index("gx"), lax.axis_index("gy"), lax.axis_index("goal")
    z, core = ig // 2, ig % 2
    xs = {-1: lax.rem(ix + nx - 1, nx), 0: ix, 1: lax.rem(ix + 1, nx)}
    ys = {-1: lax.rem(iy + ny - 1, ny), 0: iy, 1: lax.rem(iy + 1, ny)}
    partner = (ix, iy, 2 * z + (1 - core))
    z_at = [lax.rem(z + d, nz) for d in range(nz)]
    z_back = [lax.rem(z + nz - d, nz) for d in range(nz)]
    z_peer = [(ix, iy, 2 * z_at[d] + core) for d in range(nz)]
    around = [(dx, dy) for dx in (-1, 0, 1) for dy in (-1, 0, 1) if (dx, dy) != (0, 0)]
    at_top, at_bottom = ix == 0, ix == nx - 1
    at_left, at_right = iy == 0, iy == ny - 1

    barrier = pltpu.get_barrier_semaphore()
    greet = [(xs[dx], ys[dy], ig) for dx, dy in around] + [partner] + z_peer[1:]
    for device in greet:
        pl.semaphore_signal(barrier, inc=1, device_id=device, device_id_type=MESH)

    count = [0]

    def local(src, dst):
        copy = pltpu.make_async_copy(src, dst, lsem.at[count[0]])
        count[0] += 1
        copy.start()
        return copy

    body_rows = pl.ds(PAD, height)
    first, last = pl.ds(0, 8), pl.ds(height - 8, 8)
    above, below = pl.ds(PAD - 8, 8), pl.ds(bottom, 8)
    p_first, p_last = pl.ds(PAD, 8), pl.ds(bottom - 8, 8)
    cut = [pl.ds(LANES * h, LANES) for h in range(halves)]

    cost_in = [local(cost.at[:, cut[h]], Cb.at[h]) for h in range(halves)]
    cost_in += [local(obst.at[:, cut[h]], Ob.at[h]) for h in range(halves)]
    field_in = [local(pot.at[:, :, cut[h]], XA.at[:, h, body_rows]) for h in range(halves)]
    field_in += [local(dens.at[:, :, cut[h]], D.at[:, h, body_rows]) for h in range(halves)]

    sent = [0]

    def remote(src, dst, device):
        copy = pltpu.make_async_remote_copy(
            src_ref=src, dst_ref=dst, send_sem=ssem.at[sent[0]], recv_sem=rsem.at[sent[0]],
            device_id=device, device_id_type=MESH,
        )
        sent[0] += 1
        copy.start()
        return copy

    pl.semaphore_wait(barrier, len(greet))
    north, south = (xs[-1], ys[0], ig), (xs[1], ys[0], ig)
    halo = []
    for h in range(halves):
        halo.append(remote(pot.at[:, first, cut[h]], XA.at[:, h, below], north))
        halo.append(remote(pot.at[:, last, cut[h]], XA.at[:, h, above], south))
        halo.append(remote(dens.at[:, first, cut[h]], D.at[:, h, below], north))
        halo.append(remote(dens.at[:, last, cut[h]], D.at[:, h, above], south))

    lane = lax.broadcasted_iota(jnp.int32, (8, LANES), 1)
    sub = lax.broadcasted_iota(jnp.int32, (8, LANES), 0)
    slot = lane // 32
    offset = lane % 32

    for buffer in (0, 1):
        for h in range(halves):
            for g in range(goals):
                X[buffer][g, h, 0:8] = jnp.zeros((8, LANES), jnp.float32)
                X[buffer][g, h, rows_all - 8 : rows_all] = jnp.zeros((8, LANES), jnp.float32)
            St[buffer][h, 0:8] = jnp.zeros((8, LANES), jnp.float32)
            St[buffer][h, rows_all - 8 : rows_all] = jnp.zeros((8, LANES), jnp.float32)

    for copy in cost_in:
        copy.wait()

    def make_cost(i):
        for h in range(halves):
            blocked = Ob[h, tile_at(8 * i)].astype(jnp.float32)
            S[h, tile_at(PAD + 8 * i)] = (Cb[h, tile_at(8 * i)] + OBSTACLE_COST * blocked) * CELL_SIZE

    loop(0, height // 8, make_cost, unroll=2)
    halo.append(remote(S.at[:, p_first], S.at[:, below], north))
    halo.append(remote(S.at[:, p_last], S.at[:, above], south))
    for copy in field_in:
        copy.wait()

    def in_slots(tiles, shift):
        out = roll(tiles[0], shift)
        for g in range(1, len(tiles)):
            out = jnp.where(slot == g, roll(tiles[g], shift + 32 * g), out)
        return out

    def repeated(tile, shift):
        out = jnp.where(offset < 8, roll(tile, shift), 0.0)
        return out

    right_edge = 8 - LANES

    def pack(i):
        t = tile_at(PAD + 8 * i)
        tm = tile_at(8 * i)
        p = [XA[g, halves - 1, t] for g in range(goals)]
        s = [S[halves - 1, t]] * goals
        d = [D[k, halves - 1, t] for k in range(groups)]
        out = in_slots(p, right_edge)
        out = jnp.where(offset < 8, out, in_slots(s, right_edge + 8))
        MR[tm] = jnp.where(offset < 16, out, in_slots(d, right_edge + 16))
        p = [XA[g, 0, t] for g in range(goals)]
        s = [S[0, t]] * goals
        d = [D[k, 0, t] for k in range(groups)]
        out = in_slots(p, 24)
        out = jnp.where(offset >= 24, out, in_slots(s, 16))
        ML[tm] = jnp.where(offset >= 16, out, in_slots(d, 8))

    loop(0, height // 8, pack, unroll=2)

    def send_columns(mr, ml, rl, rr):
        out = [
            remote(mr, rl.at[body_rows], (xs[0], ys[1], ig)),
            remote(ml, rr.at[body_rows], (xs[0], ys[-1], ig)),
            remote(mr.at[first], rl.at[below], (xs[-1], ys[1], ig)),
            remote(mr.at[last], rl.at[above], (xs[1], ys[1], ig)),
            remote(ml.at[first], rr.at[below], (xs[-1], ys[-1], ig)),
            remote(ml.at[last], rr.at[above], (xs[1], ys[-1], ig)),
        ]
        return out

    halo += send_columns(MR, ML, RL, RR)
    for copy in halo:
        copy.wait()

    n_ext = height // 8 + 2
    own_left, own_right = offset >= 8, offset < 24

    def build(i):
        t = tile_at(PAD - 8 + 8 * i)
        from_left, from_right = RL[t], RR[t]
        s = jnp.where(own_left, in_slots([S[0, t]] * goals, 8), roll(from_left, -8))
        s_left = jnp.where(at_left & ~own_left, SHUT, s)
        p = jnp.where(own_left, in_slots([XA[g, 0, t] for g in range(goals)], 8), from_left)
        SA[0, t] = jnp.where(at_left & ~own_left, FAR - roll(s, -1), p)
        Ss[0, t] = s_left
        Ds[0, t] = jnp.where(
            own_left, in_slots([D[k, 0, t] for k in range(groups)], 8), roll(from_left, -16)
        )
        shift = 24 - LANES
        s = jnp.where(own_right, in_slots([S[halves - 1, t]] * goals, shift), roll(from_right, 8))
        s_right = jnp.where(at_right & ~own_right, SHUT, s)
        p = jnp.where(
            own_right, in_slots([XA[g, halves - 1, t] for g in range(goals)], shift), from_right
        )
        SA[1, t] = jnp.where(at_right & ~own_right, FAR - roll(s, 1), p)
        Ss[1, t] = s_right
        Ds[1, t] = jnp.where(
            own_right, in_slots([D[k, halves - 1, t] for k in range(groups)], shift), roll(from_right, 16)
        )

    loop(0, n_ext, build, unroll=U_BUILD)

    for flag, ghost, inner in ((at_top, above, PAD), (at_bottom, below, bottom - 1)):
        for h in range(halves):
            beside = jnp.broadcast_to(FAR - S[h, inner : inner + 1], (8, LANES))
            for g in range(goals):
                XA[g, h, ghost] = jnp.where(flag, beside, XA[g, h, ghost])
            S[h, ghost] = jnp.where(flag, SHUT, S[h, ghost])
        for side in (0, 1):
            beside = Ss[side, inner : inner + 1]
            beside = jnp.where(beside < SHUT, FAR - beside, FAR)
            beside = jnp.broadcast_to(beside, (8, LANES))
            SA[side, ghost] = jnp.where(flag, beside, SA[side, ghost])
            Ss[side, ghost] = jnp.where(flag, SHUT, Ss[side, ghost])

    width_all = width * ny
    cell = sub * width + lane
    target, strip_row = [], [jnp.full((8, LANES), -1000, jnp.int32) for _ in (0, 1)]
    for g in range(goals):
        row = dest[g] // width_all - ix * height
        col = dest[g] % width_all - iy * width
        held = (col >= 0) & (col < width)
        target.append(jnp.where(held, row * width + col, -(1 << 24)))
        for side, start in ((0, -8), (1, width - 24)):
            here = (slot == g) & (offset + start == col)
            strip_row[side] = jnp.where(here, row, strip_row[side])

    def relax(centre, up, down, left, right, s):
        return soft_min([centre, up + s, down + s, left + s, right + s], K_SWEEP, SWEEP_TEMP)

    def sweep(now, later, lo, hi):
        def tile(i):
            base = PAD - 8 + 8 * i
            t, tu, td = tile_at(base), pl.ds(base - 1, 8), pl.ds(base + 1, 8)
            row = 8 * i - 8
            s = [S[h, t] for h in range(halves)]
            for g in range(goals):
                centre = [X[now][g, h, t] for h in range(halves)]
                to_right = [roll(c, 1) for c in centre]
                to_left = [roll(c, -1) for c in centre]
                for h in range(halves):
                    left, right = to_right[h], to_left[h]
                    if h > 0:
                        left = jnp.where(lane == 0, to_right[h - 1], left)
                    if h < halves - 1:
                        right = jnp.where(lane == LANES - 1, to_left[h + 1], right)
                    new = relax(centre[h], X[now][g, h, tu], X[now][g, h, td], left, right, s[h])
                    pinned = cell == target[g] - (row * width + LANES * h)
                    X[later][g, h, t] = jnp.where(pinned, 0.0, new)
            for side in (0, 1):
                c = St[now][side, t]
                new = relax(c, St[now][side, tu], St[now][side, td], roll(c, 1), roll(c, -1), Ss[side, t])
                St[later][side, t] = jnp.where(strip_row[side] == sub + row, 0.0, new)

        loop(lo, hi, tile, unroll=U_SWEEP)

    def two_sweeps(j):
        sweep(0, 1, 0, n_ext)
        sweep(1, 0, 0, n_ext)

    loop(0, SWEEPS // 2, two_sweeps)

    bias = [[jnp.where(gid[g] == k, 0.0, ABSENT) for k in range(groups)] for g in range(goals)]

    def merged(main, left, right, g, h):
        if h == 0:
            main = jnp.where(lane < 8, roll(left, -(32 * g + 8)), main)
        if h == halves - 1:
            main = jnp.where(lane >= LANES - 8, roll(right, LANES - 24 - 32 * g), main)
        return main

    def finish(i):
        t = tile_at(PAD + 8 * i)
        strips = [SA[side, t] for side in (0, 1)]
        for h in range(halves):
            p = [merged(XA[g, h, t], strips[0], strips[1], g, h) for g in range(goals)]
            for g in range(goals):
                XA[g, h, t] = p[g]
            for k in range(groups):
                G[k, h, tile_at(8 * i)] = soft_min(
                    [p[g] + bias[g][k] for g in range(goals)], K_GOAL, GOAL_TEMP
                )

    parts = 2
    part = height // parts
    tiles = part // 8
    outs, swap, spread, gather, forward = [], [], [], [], []

    def part_rows(q):
        return pl.ds(part * q, part)

    for q in range(parts):
        loop(tiles * q, tiles * (q + 1), finish, unroll=U_FIN)
        swap.append(remote(G.at[:, 1 - core, part_rows(q)], G2.at[:, part_rows(q)], partner))
    outs += [local(XA.at[:, h, body_rows], pot_out.at[:, :, cut[h]]) for h in range(halves)]

    def join(i):
        t = tile_at(8 * i)
        for k in range(groups):
            H[k, t] = soft_min([G[k, core, t], G2[k, t]], K_GOAL, GOAL_TEMP)

    chunk = part // nz

    def block(q, j):
        return pl.ds(pl.multiple_of(part * q + chunk * j, 8), chunk)

    order = sorted(range(1, nz), key=lambda d: -min(d, nz - d))
    for q in range(parts):
        swap[q].wait_recv()
        loop(tiles * q, tiles * (q + 1), join, unroll=2)
        spread.append([remote(H.at[:, block(q, z_at[d])], R.at[q, d], z_peer[d]) for d in order])

    def mine(q, j):
        return F.at[:, core, pl.ds(pl.multiple_of(PAD + part * q + chunk * j, 8), chunk)]

    for q in range(parts):
        for copy in spread[q]:
            copy.wait_recv()
        for k in range(groups):
            for i in range(chunk // 8):
                row = part * q + chunk * z + 8 * i
                items = [H[k, tile_at(row)]]
                items += [R[q, d, k, 8 * i : 8 * i + 8] for d in range(1, nz)]
                F[k, core, tile_at(PAD + row)] = soft_min(items, K_GOAL, GOAL_TEMP)
        gather.append({d: remote(mine(q, z), mine(q, z), z_peer[d]) for d in order})
        forward.append(remote(mine(q, z), mine(q, z), partner))

    def pack_field(i):
        t = tile_at(PAD + 8 * i)
        FMR[tile_at(8 * i)] = in_slots([F[k, halves - 1, t] for k in range(groups)], right_edge)
        FML[tile_at(8 * i)] = in_slots([F[k, 0, t] for k in range(groups)], 24)

    arrived = []
    for q in range(parts):
        for d in order[::-1]:
            gather[q][d].wait_recv()
            arrived.append(remote(mine(q, z_back[d]), mine(q, z_back[d]), partner))
    for q in range(parts):
        forward[q].wait_recv()
        for copy in arrived[q * (nz - 1) : (q + 1) * (nz - 1)]:
            copy.wait_recv()
        loop(tiles * q, tiles * (q + 1), pack_field, unroll=4)

    halo = [
        remote(F.at[:, :, p_first], F.at[:, :, below], north),
        remote(F.at[:, :, p_last], F.at[:, :, above], south),
    ]
    halo += send_columns(FMR, FML, FRL, FRR)
    for copy in swap + forward + arrived:
        copy.wait_send()
    for q in range(parts):
        for copy in spread[q] + list(gather[q].values()):
            copy.wait_send()

    inv_two_cells = 1.0 / (2.0 * CELL_SIZE)

    def flow(up, down, left, right, speed):
        gx = (down - up) * inv_two_cells
        gy = (right - left) * inv_two_cells
        scale = speed * lax.rsqrt(1.0 + gx * gx + gy * gy)
        return -scale * gx, -scale * gy

    def sides(row, h):
        left, right = roll(row[h], 1), roll(row[h], -1)
        if h > 0:
            left = jnp.where(lane == 0, roll(row[h - 1], 1), left)
        if h < halves - 1:
            right = jnp.where(lane == LANES - 1, roll(row[h + 1], -1), right)
        return left, right

    def three(base):
        return tile_at(base), pl.ds(base - 1, 8), pl.ds(base + 1, 8)

    def flows(i):
        t, tu, td = three(PAD - 8 + 8 * i)
        speed = []
        for h in range(halves):
            total = functools.reduce(jnp.add, [D[k, h, t] for k in range(groups)])
            speed.append(1.0 / (1.0 + total))
        for k in range(groups):
            centre = [F[k, h, t] for h in range(halves)]
            for h in range(halves):
                left, right = sides(centre, h)
                Vx[k, h, t], Vy[k, h, t] = flow(F[k, h, tu], F[k, h, td], left, right, speed[h])

    def strip_flows(i):
        t, tu, td = three(PAD - 8 + 8 * i)
        for side in (0, 1):
            d = Ds[side, t]
            d = d + roll(d, 32)
            d = d + roll(d, 64)
            c = Fs[side, t]
            Vxs[side, t], Vys[side, t] = flow(
                Fs[side, tu], Fs[side, td], roll(c, 1), roll(c, -1), 1.0 / (1.0 + d)
            )

    def flux(low_v, high_v, low_d, high_d):
        face = 0.5 * (low_v + high_v)
        return jnp.maximum(face, 0.0) * low_d + jnp.minimum(face, 0.0) * high_d

    def updated(i, vx, vxu, vxd, vy, vyl, vyr, d, du, dd, dl, dr, no_left, no_right):
        row = sub + 8 * i
        up = jnp.where(at_top & (row == 0), 0.0, flux(vxu, vx, du, d))
        down = jnp.where(at_bottom & (row == height - 1), 0.0, flux(vx, vxd, d, dd))
        left, right = flux(vyl, vy, dl, d), flux(vy, vyr, d, dr)
        left = left if no_left is None else jnp.where(no_left, 0.0, left)
        right = right if no_right is None else jnp.where(no_right, 0.0, right)
        return d - COURANT * (down - up + right - left)

    def advect(i):
        t, tu, td = three(PAD + 8 * i)
        for k in range(groups):
            vy = [Vy[k, h, t] for h in range(halves)]
            d = [D[k, h, t] for h in range(halves)]
            for h in range(halves):
                vyl, vyr = sides(vy, h)
                dl, dr = sides(d, h)
                DO[k, h, tile_at(8 * i)] = updated(
                    i, Vx[k, h, t], Vx[k, h, tu], Vx[k, h, td], vy[h], vyl, vyr,
                    d[h], D[k, h, tu], D[k, h, td], dl, dr, None, None,
                )

    def strip_advect(i):
        t, tu, td = three(PAD + 8 * i)
        to = tile_at(8 * i)
        strips = []
        for side in (0, 1):
            vx, vy, d = Vxs[side, t], Vys[side, t], Ds[side, t]
            new = updated(
                i, vx, Vxs[side, tu], Vxs[side, td], vy, roll(vy, 1), roll(vy, -1),
                d, Ds[side, tu], Ds[side, td], roll(d, 1), roll(d, -1),
                (at_left & (offset == 8)) if side == 0 else None,
                (at_right & (offset == 23)) if side == 1 else None,
            )
            strips.append((vx, vy, new))
        for k in range(groups):
            for h in range(halves):
                Vx[k, h, t] = merged(Vx[k, h, t], strips[0][0], strips[1][0], k, h)
                Vy[k, h, t] = merged(Vy[k, h, t], strips[0][1], strips[1][1], k, h)
                DO[k, h, to] = merged(DO[k, h, to], strips[0][2], strips[1][2], k, h)

    loop(2, n_ext - 2, flows, unroll=2)
    loop(2, height // 8 - 2, advect, unroll=2)
    for copy in halo:
        copy.wait()

    for flag, ghost, inner in ((at_top, above, PAD), (at_bottom, below, bottom - 1)):
        for h in range(halves):
            for k in range(groups):
                beside = jnp.broadcast_to(F[k, h, inner : inner + 1], (8, LANES))
                F[k, h, ghost] = jnp.where(flag, beside, F[k, h, ghost])

    def build_field(i):
        t = tile_at(PAD - 8 + 8 * i)
        f = jnp.where(own_left, in_slots([F[k, 0, t] for k in range(groups)], 8), FRL[t])
        Fs[0, t] = jnp.where(at_left & ~own_left, roll(f, -1), f)
        f = jnp.where(
            own_right, in_slots([F[k, halves - 1, t] for k in range(groups)], 24 - LANES), FRR[t]
        )
        Fs[1, t] = jnp.where(at_right & ~own_right, roll(f, 1), f)

    loop(0, n_ext, build_field, unroll=6)
    for flag, ghost, inner in ((at_top, above, PAD), (at_bottom, below, bottom - 1)):
        for side in (0, 1):
            beside = jnp.broadcast_to(Fs[side, inner : inner + 1], (8, LANES))
            Fs[side, ghost] = jnp.where(flag, beside, Fs[side, ghost])
    loop(0, n_ext, strip_flows, unroll=6)
    for i in (0, 1, n_ext - 2, n_ext - 1):
        flows(i)
    for i in (0, 1, height // 8 - 2, height // 8 - 1):
        advect(i)
    for q in range(parts):
        loop(tiles * q, tiles * (q + 1), strip_advect, unroll=2)
        rows, here = pl.ds(PAD + part * q, part), part_rows(q)
        for h in range(halves):
            outs.append(local(Vx.at[:, h, rows], vel_out.at[:, 0, here, cut[h]]))
            outs.append(local(Vy.at[:, h, rows], vel_out.at[:, 1, here, cut[h]]))
            outs.append(local(DO.at[:, h, here], den_out.at[:, here, cut[h]]))
    for copy in outs:
        copy.wait()


def solution(mesh):
    nx, ny, ng = mesh.shape["gx"], mesh.shape["gy"], mesh.shape["goal"]

    def per_device(potential, cost, obstacle, density, destinations, group_ids):
        goals, height, width = potential.shape
        groups = density.shape[0]
        halves = width // LANES
        rows = height + 2 * PAD
        nz = ng // 2
        f32 = jnp.float32

        def vm(*shape, dtype=f32):
            return pltpu.VMEM(shape, dtype)

        panel = (rows, LANES)
        flat = (height, LANES)
        scratch = [
            vm(goals, halves, *panel), vm(goals, halves, *panel), vm(2, *panel), vm(2, *panel), vm(halves, *panel), vm(2, *panel),
            vm(halves, *flat), vm(halves, *flat, dtype=jnp.int32),
            vm(groups, halves, *panel), vm(2, *panel), vm(*flat), vm(*flat), vm(*panel), vm(*panel),
            vm(groups, halves, *flat), vm(groups, *flat), vm(groups, *flat),
            vm(2, nz, groups, height // (2 * nz), LANES), vm(groups, halves, *panel), vm(2, *panel),
            vm(*flat), vm(*flat), vm(*panel), vm(*panel),
            vm(groups, halves, *panel), vm(groups, halves, *panel), vm(2, *panel), vm(2, *panel),
            vm(groups, halves, *flat),
            pltpu.SemaphoreType.DMA((32,)),
            pltpu.SemaphoreType.DMA((80,)),
            pltpu.SemaphoreType.DMA((80,)),
        ]
        anywhere = pl.BlockSpec(memory_space=pltpu.HBM)
        scalars = pl.BlockSpec(memory_space=pltpu.SMEM)
        return pl.pallas_call(
            functools.partial(kernel, nx, ny, nz, goals, groups, height, width),
            out_shape=(
                jax.ShapeDtypeStruct(potential.shape, f32),
                jax.ShapeDtypeStruct((groups, 2, height, width), f32),
                jax.ShapeDtypeStruct(density.shape, f32),
            ),
            in_specs=[anywhere] * 4 + [scalars] * 2,
            out_specs=(anywhere,) * 3,
            scratch_shapes=scratch,
            compiler_params=pltpu.CompilerParams(
                collective_id=0, has_side_effects=True, vmem_limit_bytes=67043328
            ),
            name="crowd_step",
        )(potential, cost, obstacle, density, destinations, group_ids)

    in_specs = (
        P("goal", "gx", "gy"),
        P("gx", "gy"),
        P("gx", "gy"),
        P(None, "gx", "gy"),
        P("goal"),
        P("goal"),
    )
    out_specs = (P("goal", "gx", "gy"), P(None, None, "gx", "gy"), P(None, "gx", "gy"))
    return jax.shard_map(
        per_device, mesh=mesh, in_specs=in_specs, out_specs=out_specs, check_vma=False
    )
```

```python
import functools

import jax
import jax.numpy as jnp
import numpy as np
from jax import lax
from jax.experimental import pallas as pl
from jax.experimental.pallas import tpu as pltpu
from jax.sharding import PartitionSpec as P

MESH = pl.DeviceIdType.MESH
SWEEPS = 8
CELL_SIZE = 0.005
SWEEP_TEMP = 0.002
GOAL_TEMP = 0.01
OBSTACLE_COST = 8.0
COURANT = 0.4
FAR = 10000.0
SHUT = 1e30
ABSENT = 1e28

LANES = 128
PAD = 16
U_SWEEP, U_BUILD, U_FIN = 9, 3, 4
VMEM_LIMIT = 67043328 - (2 << 20) - (64 << 10)
K_SWEEP = float(1.0 / (SWEEP_TEMP * np.log(2.0)))
K_GOAL = float(1.0 / (GOAL_TEMP * np.log(2.0)))


def roll(x, shift):
    shift %= LANES
    return x if shift == 0 else pltpu.roll(x, shift, 1)


def soft_min(items, k, temp):
    least = functools.reduce(jnp.minimum, items)
    total = functools.reduce(jnp.add, [jnp.exp2((least - item) * k) for item in items])
    return least - temp * jnp.log(total)


def loop(start, stop, body, unroll=1):
    def step(i, carry):
        body(i)
        return carry

    lax.fori_loop(start, stop, step, 0, unroll=unroll)


def tile_at(row):
    return pl.ds(pl.multiple_of(row, 8), 8)


def kernel(
    nx, ny, nz, goals, groups, height, width,
    pot, cost, obst, dens, dest, gid,
    pot_out, vel_out, den_out,
    XA, XB, SA, SB, S, Ss, Cb, Ob, D, Ds, ML, MR, RL, RR,
    G, G2, H, R, F, Fs, FML, FMR, FRL, FRR, Vx, Vy, Vxs, Vys, DO,
    lsem, ssem, rsem,
):
    X, St = (XA, XB), (SA, SB)
    halves = width // LANES
    rows_all = height + 2 * PAD
    bottom = PAD + height
    ix, iy, ig = lax.axis_index("gx"), lax.axis_index("gy"), lax.axis_index("goal")
    z, core = ig // 2, ig % 2
    xs = {-1: lax.rem(ix + nx - 1, nx), 0: ix, 1: lax.rem(ix + 1, nx)}
    ys = {-1: lax.rem(iy + ny - 1, ny), 0: iy, 1: lax.rem(iy + 1, ny)}
    partner = (ix, iy, 2 * z + (1 - core))
    z_at = [lax.rem(z + d, nz) for d in range(nz)]
    z_back = [lax.rem(z + nz - d, nz) for d in range(nz)]
    z_peer = [(ix, iy, 2 * z_at[d] + core) for d in range(nz)]
    around = [(dx, dy) for dx in (-1, 0, 1) for dy in (-1, 0, 1) if (dx, dy) != (0, 0)]
    at_top, at_bottom = ix == 0, ix == nx - 1
    at_left, at_right = iy == 0, iy == ny - 1

    barrier = pltpu.get_barrier_semaphore()
    greet = [(xs[dx], ys[dy], ig) for dx, dy in around] + [partner] + z_peer[1:]
    for device in greet:
        pl.semaphore_signal(barrier, inc=1, device_id=device, device_id_type=MESH)

    count = [0]

    def local(src, dst):
        copy = pltpu.make_async_copy(src, dst, lsem.at[count[0]])
        count[0] += 1
        copy.start()
        return copy

    body_rows = pl.ds(PAD, height)
    first, last = pl.ds(0, 8), pl.ds(height - 8, 8)
    above, below = pl.ds(PAD - 8, 8), pl.ds(bottom, 8)
    p_first, p_last = pl.ds(PAD, 8), pl.ds(bottom - 8, 8)
    cut = [pl.ds(LANES * h, LANES) for h in range(halves)]

    cost_in = [local(cost.at[:, cut[h]], Cb.at[h]) for h in range(halves)]
    cost_in += [local(obst.at[:, cut[h]], Ob.at[h]) for h in range(halves)]
    field_in = [local(pot.at[:, :, cut[h]], XA.at[:, h, body_rows]) for h in range(halves)]
    field_in += [local(dens.at[:, :, cut[h]], D.at[:, h, body_rows]) for h in range(halves)]

    sent = [0]

    def remote(src, dst, device):
        copy = pltpu.make_async_remote_copy(
            src_ref=src, dst_ref=dst, send_sem=ssem.at[sent[0]], recv_sem=rsem.at[sent[0]],
            device_id=device, device_id_type=MESH,
        )
        sent[0] += 1
        copy.start()
        return copy

    pl.semaphore_wait(barrier, len(greet))
    north, south = (xs[-1], ys[0], ig), (xs[1], ys[0], ig)
    halo = []
    for h in range(halves):
        halo.append(remote(pot.at[:, first, cut[h]], XA.at[:, h, below], north))
        halo.append(remote(pot.at[:, last, cut[h]], XA.at[:, h, above], south))

    lane = lax.broadcasted_iota(jnp.int32, (8, LANES), 1)
    sub = lax.broadcasted_iota(jnp.int32, (8, LANES), 0)
    slot = lane // 32
    offset = lane % 32

    for buffer in (0, 1):
        for h in range(halves):
            for g in range(goals):
                X[buffer][g, h, 0:8] = jnp.zeros((8, LANES), jnp.float32)
                X[buffer][g, h, rows_all - 8 : rows_all] = jnp.zeros((8, LANES), jnp.float32)
            St[buffer][h, 0:8] = jnp.zeros((8, LANES), jnp.float32)
            St[buffer][h, rows_all - 8 : rows_all] = jnp.zeros((8, LANES), jnp.float32)

    for copy in cost_in:
        copy.wait()

    def make_cost(i):
        for h in range(halves):
            blocked = Ob[h, tile_at(8 * i)].astype(jnp.float32)
            S[h, tile_at(PAD + 8 * i)] = (Cb[h, tile_at(8 * i)] + OBSTACLE_COST * blocked) * CELL_SIZE

    loop(0, height // 8, make_cost, unroll=2)
    halo.append(remote(S.at[:, p_first], S.at[:, below], north))
    halo.append(remote(S.at[:, p_last], S.at[:, above], south))
    for copy in field_in:
        copy.wait()

    def in_slots(tiles, shift):
        out = roll(tiles[0], shift)
        for g in range(1, len(tiles)):
            out = jnp.where(slot == g, roll(tiles[g], shift + 32 * g), out)
        return out

    def repeated(tile, shift):
        out = jnp.where(offset < 8, roll(tile, shift), 0.0)
        return out

    right_edge = 8 - LANES

    def pack(i):
        t = tile_at(PAD + 8 * i)
        tm = tile_at(8 * i)
        p = [XA[g, halves - 1, t] for g in range(goals)]
        s = [S[halves - 1, t]] * goals
        d = [D[k, halves - 1, t] for k in range(groups)]
        out = in_slots(p, right_edge)
        out = jnp.where(offset < 8, out, in_slots(s, right_edge + 8))
        MR[tm] = jnp.where(offset < 16, out, in_slots(d, right_edge + 16))
        p = [XA[g, 0, t] for g in range(goals)]
        s = [S[0, t]] * goals
        d = [D[k, 0, t] for k in range(groups)]
        out = in_slots(p, 24)
        out = jnp.where(offset >= 24, out, in_slots(s, 16))
        ML[tm] = jnp.where(offset >= 16, out, in_slots(d, 8))

    loop(0, height // 8, pack, unroll=2)

    def send_columns(mr, ml, rl, rr):
        out = [
            remote(mr, rl.at[body_rows], (xs[0], ys[1], ig)),
            remote(ml, rr.at[body_rows], (xs[0], ys[-1], ig)),
            remote(mr.at[first], rl.at[below], (xs[-1], ys[1], ig)),
            remote(mr.at[last], rl.at[above], (xs[1], ys[1], ig)),
            remote(ml.at[first], rr.at[below], (xs[-1], ys[-1], ig)),
            remote(ml.at[last], rr.at[above], (xs[1], ys[-1], ig)),
        ]
        return out

    halo += send_columns(MR, ML, RL, RR)
    late = []
    for h in range(halves):
        late.append(remote(dens.at[:, first, cut[h]], D.at[:, h, below], north))
        late.append(remote(dens.at[:, last, cut[h]], D.at[:, h, above], south))

    n_ext = height // 8 + 2
    own_left, own_right = offset >= 8, offset < 24

    def build_own(i):
        t = tile_at(PAD - 8 + 8 * i)
        SA[0, t] = in_slots([XA[g, 0, t] for g in range(goals)], 8)
        SA[1, t] = in_slots([XA[g, halves - 1, t] for g in range(goals)], 24 - LANES)

    def build(i):
        t = tile_at(PAD - 8 + 8 * i)
        from_left, from_right = RL[t], RR[t]
        s = jnp.where(own_left, in_slots([S[0, t]] * goals, 8), roll(from_left, -8))
        s_left = jnp.where(at_left & ~own_left, SHUT, s)
        p = jnp.where(own_left, SA[0, t], from_left)
        SA[0, t] = jnp.where(at_left & ~own_left, FAR - roll(s, -1), p)
        Ss[0, t] = s_left
        shift = 24 - LANES
        s = jnp.where(own_right, in_slots([S[halves - 1, t]] * goals, shift), roll(from_right, 8))
        s_right = jnp.where(at_right & ~own_right, SHUT, s)
        p = jnp.where(own_right, SA[1, t], from_right)
        SA[1, t] = jnp.where(at_right & ~own_right, FAR - roll(s, 1), p)
        Ss[1, t] = s_right

    width_all = width * ny
    cell = sub * width + lane
    target, strip_row = [], [jnp.full((8, LANES), -1000, jnp.int32) for _ in (0, 1)]
    for g in range(goals):
        row = dest[g] // width_all - ix * height
        col = dest[g] % width_all - iy * width
        held = (col >= 0) & (col < width)
        target.append(jnp.where(held, row * width + col, -(1 << 24)))
        for side, start in ((0, -8), (1, width - 24)):
            here = (slot == g) & (offset + start == col)
            strip_row[side] = jnp.where(here, row, strip_row[side])

    def relax(centre, up, down, left, right, s):
        return soft_min([centre, up + s, down + s, left + s, right + s], K_SWEEP, SWEEP_TEMP)

    def three(base):
        return tile_at(base), pl.ds(base - 1, 8), pl.ds(base + 1, 8)

    def sweep(number, lo, hi, main, strips):
        now, later = (number - 1) % 2, number % 2

        def tile(i):
            t, tu, td = three(PAD - 8 + 8 * i)
            row = 8 * i - 8
            if main:
                s = [S[h, t] for h in range(halves)]
                for g in range(goals):
                    centre = [X[now][g, h, t] for h in range(halves)]
                    to_right = [roll(c, 1) for c in centre]
                    to_left = [roll(c, -1) for c in centre]
                    for h in range(halves):
                        left, right = to_right[h], to_left[h]
                        if h > 0:
                            left = jnp.where(lane == 0, to_right[h - 1], left)
                        if h < halves - 1:
                            right = jnp.where(lane == LANES - 1, to_left[h + 1], right)
                        new = relax(centre[h], X[now][g, h, tu], X[now][g, h, td], left, right, s[h])
                        pinned = cell == target[g] - (row * width + LANES * h)
                        X[later][g, h, t] = jnp.where(pinned, 0.0, new)
            if strips:
                for side in (0, 1):
                    c = St[now][side, t]
                    new = relax(
                        c, St[now][side, tu], St[now][side, td], roll(c, 1), roll(c, -1), Ss[side, t]
                    )
                    St[later][side, t] = jnp.where(strip_row[side] == sub + row, 0.0, new)

        if hi > lo:
            loop(lo, hi, tile, unroll=hi - lo)

    loop(1, n_ext - 1, build_own, unroll=4)
    early = 3
    for number in range(1, early + 1):
        sweep(number, number + 1, n_ext - 1 - number, True, False)
    for copy in halo:
        copy.wait()
    build_own(0)
    build_own(n_ext - 1)
    loop(0, n_ext, build, unroll=U_BUILD)

    for flag, ghost, inner in ((at_top, above, PAD), (at_bottom, below, bottom - 1)):
        for h in range(halves):
            beside = jnp.broadcast_to(FAR - S[h, inner : inner + 1], (8, LANES))
            for g in range(goals):
                XA[g, h, ghost] = jnp.where(flag, beside, XA[g, h, ghost])
            S[h, ghost] = jnp.where(flag, SHUT, S[h, ghost])
        for side in (0, 1):
            beside = Ss[side, inner : inner + 1]
            beside = jnp.where(beside < SHUT, FAR - beside, FAR)
            beside = jnp.broadcast_to(beside, (8, LANES))
            SA[side, ghost] = jnp.where(flag, beside, SA[side, ghost])
            Ss[side, ghost] = jnp.where(flag, SHUT, Ss[side, ghost])

    for number in range(1, SWEEPS + 1):
        start, stop = (1 if number == SWEEPS else 0), n_ext - 1 - number
        if number <= early:
            sweep(number, start, number + 1, True, True)
            sweep(number, number + 1, stop, False, True)
        else:
            sweep(number, start, stop, True, True)

    def lower(number):
        sweep(number, n_ext - 1 - number, n_ext - (1 if number == SWEEPS else 0), True, True)

    bias = [[jnp.where(gid[g] == k, 0.0, ABSENT) for k in range(groups)] for g in range(goals)]

    def merged(main, left, right, g, h):
        if h == 0:
            main = jnp.where(lane < 8, roll(left, -(32 * g + 8)), main)
        if h == halves - 1:
            main = jnp.where(lane >= LANES - 8, roll(right, LANES - 24 - 32 * g), main)
        return main

    def finish(i):
        t = tile_at(PAD + 8 * i)
        strips = [SA[side, t] for side in (0, 1)]
        for h in range(halves):
            p = [merged(XA[g, h, t], strips[0], strips[1], g, h) for g in range(goals)]
            for g in range(goals):
                pot_out[g, tile_at(8 * i), cut[h]] = p[g]
            for k in range(groups):
                G[k, h, tile_at(8 * i)] = soft_min(
                    [p[g] + bias[g][k] for g in range(goals)], K_GOAL, GOAL_TEMP
                )

    parts = 2
    part = height // parts
    tiles = part // 8
    swap, spread, gather, forward = [], [], [], []

    def part_rows(q):
        return pl.ds(part * q, part)

    def finish_part(q):
        loop(tiles * q, tiles * (q + 1), finish, unroll=U_FIN)
        swap.append(remote(G.at[:, 1 - core, part_rows(q)], G2.at[:, part_rows(q)], partner))


    def join(i):
        t = tile_at(8 * i)
        for k in range(groups):
            H[k, t] = soft_min([G[k, core, t], G2[k, t]], K_GOAL, GOAL_TEMP)

    chunk = part // nz

    def block(q, j):
        return pl.ds(pl.multiple_of(part * q + chunk * j, 8), chunk)

    order = sorted(range(1, nz), key=lambda d: -min(d, nz - d))
    finish_part(0)
    for number in range(1, SWEEPS - 1):
        lower(number)
    for q in range(parts):
        swap[q].wait_recv()
        loop(tiles * q, tiles * (q + 1), join, unroll=4)
        spread.append([remote(H.at[:, block(q, z_at[d])], R.at[q, d], z_peer[d]) for d in order])
        if q == 0:
            lower(SWEEPS - 1)
            lower(SWEEPS)
            finish_part(1)

    def mine(q, j):
        return F.at[:, core, pl.ds(pl.multiple_of(PAD + part * q + chunk * j, 8), chunk)]

    for q in range(parts):
        for copy in spread[q]:
            copy.wait_recv()
        for k in range(groups):
            for i in range(chunk // 8):
                row = part * q + chunk * z + 8 * i
                items = [H[k, tile_at(row)]]
                items += [R[q, d, k, 8 * i : 8 * i + 8] for d in range(1, nz)]
                F[k, core, tile_at(PAD + row)] = soft_min(items, K_GOAL, GOAL_TEMP)
        gather.append({d: remote(mine(q, z), mine(q, z), z_peer[d]) for d in order})
        forward.append(remote(mine(q, z), mine(q, z), partner))

    def pack_field(i):
        t = tile_at(PAD + 8 * i)
        FMR[tile_at(8 * i)] = in_slots([F[k, halves - 1, t] for k in range(groups)], right_edge)
        FML[tile_at(8 * i)] = in_slots([F[k, 0, t] for k in range(groups)], 24)

    arrived = []
    for q in range(parts):
        for d in order[::-1]:
            gather[q][d].wait_recv()
            arrived.append(remote(mine(q, z_back[d]), mine(q, z_back[d]), partner))
    for q in range(parts):
        forward[q].wait_recv()
        for copy in arrived[q * (nz - 1) : (q + 1) * (nz - 1)]:
            copy.wait_recv()
        loop(tiles * q, tiles * (q + 1), pack_field, unroll=4)

    halo = [
        remote(F.at[:, :, p_first], F.at[:, :, below], north),
        remote(F.at[:, :, p_last], F.at[:, :, above], south),
    ]
    halo += send_columns(FMR, FML, FRL, FRR)
    for copy in swap + forward + arrived:
        copy.wait_send()
    for q in range(parts):
        for copy in spread[q] + list(gather[q].values()):
            copy.wait_send()

    inv_two_cells = 1.0 / (2.0 * CELL_SIZE)

    def flow(up, down, left, right, speed):
        gx = (down - up) * inv_two_cells
        gy = (right - left) * inv_two_cells
        scale = speed * lax.rsqrt(1.0 + gx * gx + gy * gy)
        return -scale * gx, -scale * gy

    def sides(row, h):
        left, right = roll(row[h], 1), roll(row[h], -1)
        if h > 0:
            left = jnp.where(lane == 0, roll(row[h - 1], 1), left)
        if h < halves - 1:
            right = jnp.where(lane == LANES - 1, roll(row[h + 1], -1), right)
        return left, right

    def flows(i):
        t, tu, td = three(PAD - 8 + 8 * i)
        speed = []
        for h in range(halves):
            total = functools.reduce(jnp.add, [D[k, h, t] for k in range(groups)])
            speed.append(1.0 / (1.0 + total))
        for k in range(groups):
            centre = [F[k, h, t] for h in range(halves)]
            for h in range(halves):
                left, right = sides(centre, h)
                Vx[k, h, t], Vy[k, h, t] = flow(F[k, h, tu], F[k, h, td], left, right, speed[h])

    def strip_flows(i):
        t, tu, td = three(PAD - 8 + 8 * i)
        for side in (0, 1):
            d = Ds[side, t]
            d = d + roll(d, 32)
            d = d + roll(d, 64)
            c = Fs[side, t]
            Vxs[side, t], Vys[side, t] = flow(
                Fs[side, tu], Fs[side, td], roll(c, 1), roll(c, -1), 1.0 / (1.0 + d)
            )

    def flux(low_v, high_v, low_d, high_d):
        face = 0.5 * (low_v + high_v)
        return jnp.maximum(face, 0.0) * low_d + jnp.minimum(face, 0.0) * high_d

    def updated(i, vx, vxu, vxd, vy, vyl, vyr, d, du, dd, dl, dr, no_left, no_right):
        row = sub + 8 * i
        up = jnp.where(at_top & (row == 0), 0.0, flux(vxu, vx, du, d))
        down = jnp.where(at_bottom & (row == height - 1), 0.0, flux(vx, vxd, d, dd))
        left, right = flux(vyl, vy, dl, d), flux(vy, vyr, d, dr)
        left = left if no_left is None else jnp.where(no_left, 0.0, left)
        right = right if no_right is None else jnp.where(no_right, 0.0, right)
        return d - COURANT * (down - up + right - left)

    def advect(i):
        t, tu, td = three(PAD + 8 * i)
        for k in range(groups):
            vy = [Vy[k, h, t] for h in range(halves)]
            d = [D[k, h, t] for h in range(halves)]
            for h in range(halves):
                vyl, vyr = sides(vy, h)
                dl, dr = sides(d, h)
                DO[k, h, tile_at(8 * i)] = updated(
                    i, Vx[k, h, t], Vx[k, h, tu], Vx[k, h, td], vy[h], vyl, vyr,
                    d[h], D[k, h, tu], D[k, h, td], dl, dr, None, None,
                )

    def strip_advect(i):
        t, tu, td = three(PAD + 8 * i)
        to = tile_at(8 * i)
        strips = []
        for side in (0, 1):
            vx, vy, d = Vxs[side, t], Vys[side, t], Ds[side, t]
            new = updated(
                i, vx, Vxs[side, tu], Vxs[side, td], vy, roll(vy, 1), roll(vy, -1),
                d, Ds[side, tu], Ds[side, td], roll(d, 1), roll(d, -1),
                (at_left & (offset == 8)) if side == 0 else None,
                (at_right & (offset == 23)) if side == 1 else None,
            )
            strips.append((vx, vy, new))
        for k in range(groups):
            for h in range(halves):
                vel_out[k, 0, to, cut[h]] = merged(Vx[k, h, t], strips[0][0], strips[1][0], k, h)
                vel_out[k, 1, to, cut[h]] = merged(Vy[k, h, t], strips[0][1], strips[1][1], k, h)
                den_out[k, to, cut[h]] = merged(DO[k, h, to], strips[0][2], strips[1][2], k, h)

    def build_density(i):
        t = tile_at(PAD - 8 + 8 * i)
        own = in_slots([D[k, 0, t] for k in range(groups)], 8)
        Ds[0, t] = jnp.where(own_left, own, roll(RL[t], -16))
        own = in_slots([D[k, halves - 1, t] for k in range(groups)], 24 - LANES)
        Ds[1, t] = jnp.where(own_right, own, roll(RR[t], 16))

    loop(2, n_ext - 2, flows, unroll=2)
    loop(2, height // 8 - 2, advect, unroll=2)
    for copy in late:
        copy.wait()
    loop(0, n_ext, build_density, unroll=6)
    for copy in halo:
        copy.wait()

    for flag, ghost, inner in ((at_top, above, PAD), (at_bottom, below, bottom - 1)):
        for h in range(halves):
            for k in range(groups):
                beside = jnp.broadcast_to(F[k, h, inner : inner + 1], (8, LANES))
                F[k, h, ghost] = jnp.where(flag, beside, F[k, h, ghost])

    def build_field(i):
        t = tile_at(PAD - 8 + 8 * i)
        f = jnp.where(own_left, in_slots([F[k, 0, t] for k in range(groups)], 8), FRL[t])
        Fs[0, t] = jnp.where(at_left & ~own_left, roll(f, -1), f)
        f = jnp.where(
            own_right, in_slots([F[k, halves - 1, t] for k in range(groups)], 24 - LANES), FRR[t]
        )
        Fs[1, t] = jnp.where(at_right & ~own_right, roll(f, 1), f)

    loop(0, n_ext, build_field, unroll=6)
    for flag, ghost, inner in ((at_top, above, PAD), (at_bottom, below, bottom - 1)):
        for side in (0, 1):
            beside = jnp.broadcast_to(Fs[side, inner : inner + 1], (8, LANES))
            Fs[side, ghost] = jnp.where(flag, beside, Fs[side, ghost])
    loop(0, n_ext, strip_flows, unroll=6)
    for i in (0, 1, n_ext - 2, n_ext - 1):
        flows(i)
    for i in (0, 1, height // 8 - 2, height // 8 - 1):
        advect(i)
    loop(0, height // 8, strip_advect, unroll=2)


def solution(mesh):
    nx, ny, ng = mesh.shape["gx"], mesh.shape["gy"], mesh.shape["goal"]

    def per_device(potential, cost, obstacle, density, destinations, group_ids):
        goals, height, width = potential.shape
        groups = density.shape[0]
        halves = width // LANES
        rows = height + 2 * PAD
        nz = ng // 2
        f32 = jnp.float32

        def vm(*shape, dtype=f32):
            return pltpu.VMEM(shape, dtype)

        panel = (rows, LANES)
        flat = (height, LANES)
        scratch = [
            vm(goals, halves, *panel), vm(goals, halves, *panel), vm(2, *panel), vm(2, *panel), vm(halves, *panel), vm(2, *panel),
            vm(halves, *flat), vm(halves, *flat, dtype=jnp.int32),
            vm(groups, halves, *panel), vm(2, *panel), vm(*flat), vm(*flat), vm(*panel), vm(*panel),
            vm(groups, halves, *flat), vm(groups, *flat), vm(groups, *flat),
            vm(2, nz, groups, height // (2 * nz), LANES), vm(groups, halves, *panel), vm(2, *panel),
            vm(*flat), vm(*flat), vm(*panel), vm(*panel),
            vm(groups, halves, *panel), vm(groups, halves, *panel), vm(2, *panel), vm(2, *panel),
            vm(groups, halves, *flat),
            pltpu.SemaphoreType.DMA((32,)),
            pltpu.SemaphoreType.DMA((80,)),
            pltpu.SemaphoreType.DMA((80,)),
        ]
        anywhere = pl.BlockSpec(memory_space=pltpu.HBM)
        scalars = pl.BlockSpec(memory_space=pltpu.SMEM)
        return pl.pallas_call(
            functools.partial(kernel, nx, ny, nz, goals, groups, height, width),
            out_shape=(
                vm(*potential.shape),
                vm(groups, 2, height, width),
                vm(*density.shape),
            ),
            in_specs=[anywhere] * 4 + [scalars] * 2,
            out_specs=(pl.BlockSpec(memory_space=pltpu.VMEM),) * 3,
            scratch_shapes=scratch,
            compiler_params=pltpu.CompilerParams(
                collective_id=0, has_side_effects=True, vmem_limit_bytes=VMEM_LIMIT
            ),
            name="crowd_step",
        )(potential, cost, obstacle, density, destinations, group_ids)

    in_specs = (
        P("goal", "gx", "gy"),
        P("gx", "gy"),
        P("gx", "gy"),
        P(None, "gx", "gy"),
        P("goal"),
        P("goal"),
    )
    out_specs = (P("goal", "gx", "gy"), P(None, None, "gx", "gy"), P(None, "gx", "gy"))
    return jax.shard_map(
        per_device, mesh=mesh, in_specs=in_specs, out_specs=out_specs, check_vma=False
    )
```

```python
import functools

import jax
import jax.numpy as jnp
import numpy as np
from jax import lax
from jax.experimental import pallas as pl
from jax.experimental.pallas import tpu as pltpu
from jax.sharding import PartitionSpec as P

MESH = pl.DeviceIdType.MESH
SWEEPS = 8
CELL_SIZE = 0.005
SWEEP_TEMP = 0.002
GOAL_TEMP = 0.01
OBSTACLE_COST = 8.0
COURANT = 0.4
FAR = 10000.0
SHUT = 1e30
ABSENT = 1e28

LANES = 128
PAD = 16
U_SWEEP, U_BUILD, U_FIN = 9, 3, 4
VMEM_LIMIT = 67043328 - (2 << 20) - (64 << 10)
K_SWEEP = float(1.0 / (SWEEP_TEMP * np.log(2.0)))
K_GOAL = float(1.0 / (GOAL_TEMP * np.log(2.0)))


def roll(x, shift):
    shift %= LANES
    return x if shift == 0 else pltpu.roll(x, shift, 1)


def soft_min(items, k, temp):
    least = functools.reduce(jnp.minimum, items)
    total = functools.reduce(jnp.add, [jnp.exp2((least - item) * k) for item in items])
    return least - temp * jnp.log(total)


def loop(start, stop, body, unroll=1):
    def step(i, carry):
        body(i)
        return carry

    lax.fori_loop(start, stop, step, 0, unroll=unroll)


def tile_at(row):
    return pl.ds(pl.multiple_of(row, 8), 8)


def kernel(
    nx, ny, nz, goals, groups, height, width,
    pot, cost, obst, dens, dest_in, gid_in,
    pot_out, vel_out, den_out,
    XA, XB, SA, SB, S, Ss, Cb, Ob, D, Ds, ML, MR, RL, RR,
    G, G2, H, R, F, Fs, FML, FMR, FRL, FRR, Vx, Vy, Vxs, Vys, DO,
    dest, gid, DML, DMR, DRL, DRR, lsem, ssem, rsem,
):
    X, St = (XA, XB), (SA, SB)
    halves = width // LANES
    rows_all = height + 2 * PAD
    bottom = PAD + height
    ix, iy, ig = lax.axis_index("gx"), lax.axis_index("gy"), lax.axis_index("goal")
    z, core = ig // 2, ig % 2
    xs = {-1: lax.rem(ix + nx - 1, nx), 0: ix, 1: lax.rem(ix + 1, nx)}
    ys = {-1: lax.rem(iy + ny - 1, ny), 0: iy, 1: lax.rem(iy + 1, ny)}
    partner = (ix, iy, 2 * z + (1 - core))
    z_at = [lax.rem(z + d, nz) for d in range(nz)]
    z_back = [lax.rem(z + nz - d, nz) for d in range(nz)]
    z_peer = [(ix, iy, 2 * z_at[d] + core) for d in range(nz)]
    around = [(dx, dy) for dx in (-1, 0, 1) for dy in (-1, 0, 1) if (dx, dy) != (0, 0)]
    at_top, at_bottom = ix == 0, ix == nx - 1
    at_left, at_right = iy == 0, iy == ny - 1

    barrier = pltpu.get_barrier_semaphore()
    greet = [(xs[dx], ys[dy], ig) for dx, dy in around] + [partner] + z_peer[1:]
    for device in greet:
        pl.semaphore_signal(barrier, inc=1, device_id=device, device_id_type=MESH)

    count = [0]

    def local(src, dst):
        copy = pltpu.make_async_copy(src, dst, lsem.at[count[0]])
        count[0] += 1
        copy.start()
        return copy

    body_rows = pl.ds(PAD, height)
    first, last = pl.ds(0, 8), pl.ds(height - 8, 8)
    above, below = pl.ds(PAD - 8, 8), pl.ds(bottom, 8)
    p_first, p_last = pl.ds(PAD, 8), pl.ds(bottom - 8, 8)
    cut = [pl.ds(LANES * h, LANES) for h in range(halves)]

    cost_in = [local(cost.at[:, cut[h]], Cb.at[h]) for h in range(halves)]
    cost_in += [local(obst.at[:, cut[h]], Ob.at[h]) for h in range(halves)]
    field_in = [local(pot.at[:, :, cut[h]], XA.at[:, h, body_rows]) for h in range(halves)]
    scalars_in = [local(dest_in, dest), local(gid_in, gid)]
    density_in = [local(dens.at[:, :, cut[h]], D.at[:, h, body_rows]) for h in range(halves)]

    sent = [0]

    def remote(src, dst, device):
        copy = pltpu.make_async_remote_copy(
            src_ref=src, dst_ref=dst, send_sem=ssem.at[sent[0]], recv_sem=rsem.at[sent[0]],
            device_id=device, device_id_type=MESH,
        )
        sent[0] += 1
        copy.start()
        return copy

    pl.semaphore_wait(barrier, len(greet))
    north, south = (xs[-1], ys[0], ig), (xs[1], ys[0], ig)
    halo = []
    for h in range(halves):
        halo.append(remote(pot.at[:, first, cut[h]], XA.at[:, h, below], north))
        halo.append(remote(pot.at[:, last, cut[h]], XA.at[:, h, above], south))

    lane = lax.broadcasted_iota(jnp.int32, (8, LANES), 1)
    sub = lax.broadcasted_iota(jnp.int32, (8, LANES), 0)
    slot = lane // 32
    offset = lane % 32

    for buffer in (0, 1):
        for h in range(halves):
            for g in range(goals):
                X[buffer][g, h, 0:8] = jnp.zeros((8, LANES), jnp.float32)
                X[buffer][g, h, rows_all - 8 : rows_all] = jnp.zeros((8, LANES), jnp.float32)
            St[buffer][h, 0:8] = jnp.zeros((8, LANES), jnp.float32)
            St[buffer][h, rows_all - 8 : rows_all] = jnp.zeros((8, LANES), jnp.float32)

    for copy in cost_in:
        copy.wait()

    def make_cost(i):
        for h in range(halves):
            blocked = Ob[h, tile_at(8 * i)].astype(jnp.float32)
            S[h, tile_at(PAD + 8 * i)] = (Cb[h, tile_at(8 * i)] + OBSTACLE_COST * blocked) * CELL_SIZE

    loop(0, height // 8, make_cost, unroll=2)
    halo.append(remote(S.at[:, p_first], S.at[:, below], north))
    halo.append(remote(S.at[:, p_last], S.at[:, above], south))
    for copy in field_in:
        copy.wait()

    def in_slots(tiles, shift):
        out = roll(tiles[0], shift)
        for g in range(1, len(tiles)):
            out = jnp.where(slot == g, roll(tiles[g], shift + 32 * g), out)
        return out

    def repeated(tile, shift):
        out = jnp.where(offset < 8, roll(tile, shift), 0.0)
        return out

    right_edge = 8 - LANES

    def pack(i):
        t = tile_at(PAD + 8 * i)
        tm = tile_at(8 * i)
        p = [XA[g, halves - 1, t] for g in range(goals)]
        s = [S[halves - 1, t]] * goals
        MR[tm] = jnp.where(offset < 8, in_slots(p, right_edge), in_slots(s, right_edge + 8))
        p = [XA[g, 0, t] for g in range(goals)]
        s = [S[0, t]] * goals
        ML[tm] = jnp.where(offset >= 24, in_slots(p, 24), in_slots(s, 16))

    loop(0, height // 8, pack, unroll=4)

    def pack_columns(source, mr, ml):
        def one(i):
            t, tm = tile_at(PAD + 8 * i), tile_at(8 * i)
            mr[tm] = in_slots([source[k, halves - 1, t] for k in range(groups)], right_edge)
            ml[tm] = in_slots([source[k, 0, t] for k in range(groups)], 24)

        return one

    def send_sides(mr, ml, rl, rr, start, rows):
        here, there = pl.ds(start, rows), pl.ds(PAD + start, rows)
        return [
            remote(mr.at[here], rl.at[there], (xs[0], ys[1], ig)),
            remote(ml.at[here], rr.at[there], (xs[0], ys[-1], ig)),
        ]

    def send_corners(mr, ml, rl, rr, dx):
        here, there = (first, below) if dx < 0 else (last, above)
        return [
            remote(mr.at[here], rl.at[there], (xs[dx], ys[1], ig)),
            remote(ml.at[here], rr.at[there], (xs[dx], ys[-1], ig)),
        ]

    halo += send_sides(MR, ML, RL, RR, 0, height)
    halo += send_corners(MR, ML, RL, RR, -1) + send_corners(MR, ML, RL, RR, 1)
    late = []
    for h in range(halves):
        late.append(remote(dens.at[:, first, cut[h]], D.at[:, h, below], north))
        late.append(remote(dens.at[:, last, cut[h]], D.at[:, h, above], south))

    n_ext = height // 8 + 2
    own_left, own_right = offset >= 8, offset < 24

    def build_own(i):
        t = tile_at(PAD - 8 + 8 * i)
        SA[0, t] = in_slots([XA[g, 0, t] for g in range(goals)], 8)
        SA[1, t] = in_slots([XA[g, halves - 1, t] for g in range(goals)], 24 - LANES)

    def build(i):
        t = tile_at(PAD - 8 + 8 * i)
        from_left, from_right = RL[t], RR[t]
        s = jnp.where(own_left, in_slots([S[0, t]] * goals, 8), roll(from_left, -8))
        s_left = jnp.where(at_left & ~own_left, SHUT, s)
        p = jnp.where(own_left, SA[0, t], from_left)
        SA[0, t] = jnp.where(at_left & ~own_left, FAR - roll(s, -1), p)
        Ss[0, t] = s_left
        shift = 24 - LANES
        s = jnp.where(own_right, in_slots([S[halves - 1, t]] * goals, shift), roll(from_right, 8))
        s_right = jnp.where(at_right & ~own_right, SHUT, s)
        p = jnp.where(own_right, SA[1, t], from_right)
        SA[1, t] = jnp.where(at_right & ~own_right, FAR - roll(s, 1), p)
        Ss[1, t] = s_right

    for copy in scalars_in:
        copy.wait()
    width_all = width * ny
    cell = sub * width + lane
    target, strip_row = [], [jnp.full((8, LANES), -1000, jnp.int32) for _ in (0, 1)]
    for g in range(goals):
        row = dest[g] // width_all - ix * height
        col = dest[g] % width_all - iy * width
        held = (col >= 0) & (col < width)
        target.append(jnp.where(held, row * width + col, -(1 << 24)))
        for side, start in ((0, -8), (1, width - 24)):
            here = (slot == g) & (offset + start == col)
            strip_row[side] = jnp.where(here, row, strip_row[side])

    def relax(centre, up, down, left, right, s):
        return soft_min([centre, up + s, down + s, left + s, right + s], K_SWEEP, SWEEP_TEMP)

    def three(base):
        return tile_at(base), pl.ds(base - 1, 8), pl.ds(base + 1, 8)

    def sweep(number, lo, hi, main, strips):
        now, later = (number - 1) % 2, number % 2

        def tile(i):
            t, tu, td = three(PAD - 8 + 8 * i)
            row = 8 * i - 8
            if main:
                s = [S[h, t] for h in range(halves)]
                for g in range(goals):
                    centre = [X[now][g, h, t] for h in range(halves)]
                    to_right = [roll(c, 1) for c in centre]
                    to_left = [roll(c, -1) for c in centre]
                    for h in range(halves):
                        left, right = to_right[h], to_left[h]
                        if h > 0:
                            left = jnp.where(lane == 0, to_right[h - 1], left)
                        if h < halves - 1:
                            right = jnp.where(lane == LANES - 1, to_left[h + 1], right)
                        new = relax(centre[h], X[now][g, h, tu], X[now][g, h, td], left, right, s[h])
                        pinned = cell == target[g] - (row * width + LANES * h)
                        X[later][g, h, t] = jnp.where(pinned, 0.0, new)
            if strips:
                for side in (0, 1):
                    c = St[now][side, t]
                    new = relax(
                        c, St[now][side, tu], St[now][side, td], roll(c, 1), roll(c, -1), Ss[side, t]
                    )
                    St[later][side, t] = jnp.where(strip_row[side] == sub + row, 0.0, new)

        if hi > lo:
            loop(lo, hi, tile, unroll=hi - lo)

    loop(1, n_ext - 1, build_own, unroll=4)
    early = 3
    for number in range(1, early + 1):
        sweep(number, number + 1, n_ext - 1 - number, True, False)
    for copy in halo:
        copy.wait()
    build_own(0)
    build_own(n_ext - 1)
    loop(0, n_ext, build, unroll=U_BUILD)

    for flag, ghost, inner in ((at_top, above, PAD), (at_bottom, below, bottom - 1)):
        for h in range(halves):
            beside = jnp.broadcast_to(FAR - S[h, inner : inner + 1], (8, LANES))
            for g in range(goals):
                XA[g, h, ghost] = jnp.where(flag, beside, XA[g, h, ghost])
            S[h, ghost] = jnp.where(flag, SHUT, S[h, ghost])
        for side in (0, 1):
            beside = Ss[side, inner : inner + 1]
            beside = jnp.where(beside < SHUT, FAR - beside, FAR)
            beside = jnp.broadcast_to(beside, (8, LANES))
            SA[side, ghost] = jnp.where(flag, beside, SA[side, ghost])
            Ss[side, ghost] = jnp.where(flag, SHUT, Ss[side, ghost])

    for number in range(1, SWEEPS + 1):
        start, stop = (1 if number == SWEEPS else 0), n_ext - 1 - number
        if number <= early:
            sweep(number, start, number + 1, True, True)
            sweep(number, number + 1, stop, False, True)
        else:
            sweep(number, start, stop, True, True)

    def lower(number):
        sweep(number, n_ext - 1 - number, n_ext - (1 if number == SWEEPS else 0), True, True)

    bias = [[jnp.where(gid[g] == k, 0.0, ABSENT) for k in range(groups)] for g in range(goals)]

    def merged(main, left, right, g, h):
        if h == 0:
            main = jnp.where(lane < 8, roll(left, -(32 * g + 8)), main)
        if h == halves - 1:
            main = jnp.where(lane >= LANES - 8, roll(right, LANES - 24 - 32 * g), main)
        return main

    def finish(i):
        t = tile_at(PAD + 8 * i)
        strips = [SA[side, t] for side in (0, 1)]
        for h in range(halves):
            p = [merged(XA[g, h, t], strips[0], strips[1], g, h) for g in range(goals)]
            for g in range(goals):
                pot_out[g, tile_at(8 * i), cut[h]] = p[g]
            for k in range(groups):
                G[k, h, tile_at(8 * i)] = soft_min(
                    [p[g] + bias[g][k] for g in range(goals)], K_GOAL, GOAL_TEMP
                )

    parts = 2
    part = height // parts
    tiles = part // 8
    swap, spread, gather, forward = [], [], [], []

    def part_rows(q):
        return pl.ds(part * q, part)

    def finish_part(q):
        piece = part // 2
        moves = []
        for start in (part * q, part * q + piece):
            loop(start // 8, (start + piece) // 8, finish, unroll=U_FIN)
            rows = pl.ds(start, piece)
            moves.append(remote(G.at[:, 1 - core, rows], G2.at[:, rows], partner))
        swap.append(moves)


    def join(i):
        t = tile_at(8 * i)
        for k in range(groups):
            H[k, t] = soft_min([G[k, core, t], G2[k, t]], K_GOAL, GOAL_TEMP)

    chunk = part // nz

    def block(q, j):
        return pl.ds(pl.multiple_of(part * q + chunk * j, 8), chunk)

    order = sorted(range(1, nz), key=lambda d: -min(d, nz - d))
    finish_part(0)
    for number in range(1, SWEEPS - 1):
        lower(number)
    for q in range(parts):
        for n, copy in enumerate(swap[q]):
            copy.wait_recv()
            loop(tiles * q + tiles // 2 * n, tiles * q + tiles // 2 * (n + 1), join, unroll=4)
        spread.append([remote(H.at[:, block(q, z_at[d])], R.at[q, d], z_peer[d]) for d in order])
        if q == 0:
            lower(SWEEPS - 1)
            lower(SWEEPS)
            finish_part(1)

    for copy in density_in:
        copy.wait()
    loop(0, height // 8, pack_columns(D, DMR, DML), unroll=4)
    late += send_sides(DMR, DML, DRL, DRR, 0, height)

    def mine(q, j):
        return F.at[:, core, pl.ds(pl.multiple_of(PAD + part * q + chunk * j, 8), chunk)]

    for q in range(parts):
        for copy in spread[q]:
            copy.wait_recv()
        for k in range(groups):
            for i in range(chunk // 8):
                row = part * q + chunk * z + 8 * i
                items = [H[k, tile_at(row)]]
                items += [R[q, d, k, 8 * i : 8 * i + 8] for d in range(1, nz)]
                F[k, core, tile_at(PAD + row)] = soft_min(items, K_GOAL, GOAL_TEMP)
        gather.append({d: remote(mine(q, z), mine(q, z), z_peer[d]) for d in order})
        forward.append(remote(mine(q, z), mine(q, z), partner))

    inv_two_cells = 1.0 / (2.0 * CELL_SIZE)

    def flow(up, down, left, right, speed):
        gx = (down - up) * inv_two_cells
        gy = (right - left) * inv_two_cells
        scale = speed * lax.rsqrt(1.0 + gx * gx + gy * gy)
        return -scale * gx, -scale * gy

    def sides(row, h):
        left, right = roll(row[h], 1), roll(row[h], -1)
        if h > 0:
            left = jnp.where(lane == 0, roll(row[h - 1], 1), left)
        if h < halves - 1:
            right = jnp.where(lane == LANES - 1, roll(row[h + 1], -1), right)
        return left, right

    def flows(i):
        t, tu, td = three(PAD - 8 + 8 * i)
        speed = []
        for h in range(halves):
            total = functools.reduce(jnp.add, [D[k, h, t] for k in range(groups)])
            speed.append(1.0 / (1.0 + total))
        for k in range(groups):
            centre = [F[k, h, t] for h in range(halves)]
            for h in range(halves):
                left, right = sides(centre, h)
                Vx[k, h, t], Vy[k, h, t] = flow(F[k, h, tu], F[k, h, td], left, right, speed[h])

    def strip_flows(i):
        t, tu, td = three(PAD - 8 + 8 * i)
        for side in (0, 1):
            d = Ds[side, t]
            d = d + roll(d, 32)
            d = d + roll(d, 64)
            c = Fs[side, t]
            Vxs[side, t], Vys[side, t] = flow(
                Fs[side, tu], Fs[side, td], roll(c, 1), roll(c, -1), 1.0 / (1.0 + d)
            )

    def flux(low_v, high_v, low_d, high_d):
        face = 0.5 * (low_v + high_v)
        return jnp.maximum(face, 0.0) * low_d + jnp.minimum(face, 0.0) * high_d

    def updated(i, vx, vxu, vxd, vy, vyl, vyr, d, du, dd, dl, dr, no_left, no_right):
        row = sub + 8 * i
        up = jnp.where(at_top & (row == 0), 0.0, flux(vxu, vx, du, d))
        down = jnp.where(at_bottom & (row == height - 1), 0.0, flux(vx, vxd, d, dd))
        left, right = flux(vyl, vy, dl, d), flux(vy, vyr, d, dr)
        left = left if no_left is None else jnp.where(no_left, 0.0, left)
        right = right if no_right is None else jnp.where(no_right, 0.0, right)
        return d - COURANT * (down - up + right - left)

    def advect(i):
        t, tu, td = three(PAD + 8 * i)
        for k in range(groups):
            vy = [Vy[k, h, t] for h in range(halves)]
            d = [D[k, h, t] for h in range(halves)]
            for h in range(halves):
                vyl, vyr = sides(vy, h)
                dl, dr = sides(d, h)
                DO[k, h, tile_at(8 * i)] = updated(
                    i, Vx[k, h, t], Vx[k, h, tu], Vx[k, h, td], vy[h], vyl, vyr,
                    d[h], D[k, h, tu], D[k, h, td], dl, dr, None, None,
                )

    def strip_advect(i):
        t, tu, td = three(PAD + 8 * i)
        to = tile_at(8 * i)
        strips = []
        for side in (0, 1):
            vx, vy, d = Vxs[side, t], Vys[side, t], Ds[side, t]
            new = updated(
                i, vx, Vxs[side, tu], Vxs[side, td], vy, roll(vy, 1), roll(vy, -1),
                d, Ds[side, tu], Ds[side, td], roll(d, 1), roll(d, -1),
                (at_left & (offset == 8)) if side == 0 else None,
                (at_right & (offset == 23)) if side == 1 else None,
            )
            strips.append((vx, vy, new))
        for k in range(groups):
            for h in range(halves):
                vel_out[k, 0, to, cut[h]] = merged(Vx[k, h, t], strips[0][0], strips[1][0], k, h)
                vel_out[k, 1, to, cut[h]] = merged(Vy[k, h, t], strips[0][1], strips[1][1], k, h)
                den_out[k, to, cut[h]] = merged(DO[k, h, to], strips[0][2], strips[1][2], k, h)

    def build_density(i):
        t = tile_at(PAD - 8 + 8 * i)
        own = in_slots([D[k, 0, t] for k in range(groups)], 8)
        Ds[0, t] = jnp.where(own_left, own, DRL[t])
        own = in_slots([D[k, halves - 1, t] for k in range(groups)], 24 - LANES)
        Ds[1, t] = jnp.where(own_right, own, DRR[t])

    def build_field(i):
        t = tile_at(PAD - 8 + 8 * i)
        f = jnp.where(own_left, in_slots([F[k, 0, t] for k in range(groups)], 8), FRL[t])
        Fs[0, t] = jnp.where(at_left & ~own_left, roll(f, -1), f)
        f = jnp.where(
            own_right, in_slots([F[k, halves - 1, t] for k in range(groups)], 24 - LANES), FRR[t]
        )
        Fs[1, t] = jnp.where(at_right & ~own_right, roll(f, 1), f)

    pack_field = pack_columns(F, FMR, FML)
    halos = []

    def collect(q):
        arrived = []
        for d in order[::-1]:
            gather[q][d].wait_recv()
            arrived.append(remote(mine(q, z_back[d]), mine(q, z_back[d]), partner))
        for copy in [forward[q]] + arrived:
            copy.wait_recv()
        loop(tiles * q, tiles * (q + 1), pack_field, unroll=4)
        if q == 0:
            out = [remote(F.at[:, :, p_first], F.at[:, :, below], north)]
            out += send_corners(FMR, FML, FRL, FRR, -1)
        else:
            out = [remote(F.at[:, :, p_last], F.at[:, :, above], south)]
            out += send_corners(FMR, FML, FRL, FRR, 1)
        halos.append(out + send_sides(FMR, FML, FRL, FRR, part * q, part))
        return arrived

    passed = collect(0)
    loop(2, 8, flows, unroll=2)
    loop(2, 6, advect, unroll=2)
    passed += collect(1)
    loop(8, n_ext - 2, flows, unroll=2)
    loop(6, height // 8 - 2, advect, unroll=2)
    for copy in late:
        copy.wait()
    loop(0, n_ext, build_density, unroll=6)
    for copy in halos[0]:
        copy.wait()
    loop(1, 9, build_field, unroll=4)
    loop(2, 8, strip_flows, unroll=6)
    loop(2, 6, strip_advect, unroll=2)
    for copy in halos[1]:
        copy.wait()

    for flag, ghost, inner in ((at_top, above, PAD), (at_bottom, below, bottom - 1)):
        for h in range(halves):
            for k in range(groups):
                beside = jnp.broadcast_to(F[k, h, inner : inner + 1], (8, LANES))
                F[k, h, ghost] = jnp.where(flag, beside, F[k, h, ghost])
    build_field(0)
    loop(9, n_ext, build_field, unroll=9)
    for flag, ghost, inner in ((at_top, above, PAD), (at_bottom, below, bottom - 1)):
        for side in (0, 1):
            beside = jnp.broadcast_to(Fs[side, inner : inner + 1], (8, LANES))
            Fs[side, ghost] = jnp.where(flag, beside, Fs[side, ghost])
    for i in (0, 1, n_ext - 2, n_ext - 1):
        flows(i)
    for i in (0, 1):
        strip_flows(i)
    loop(8, n_ext, strip_flows, unroll=10)
    for i in (0, 1, height // 8 - 2, height // 8 - 1):
        advect(i)
    loop(0, 2, strip_advect, unroll=2)
    loop(6, height // 8, strip_advect, unroll=2)

    for copy in swap[0] + swap[1] + forward + passed:
        copy.wait_send()
    for q in range(parts):
        for copy in spread[q] + list(gather[q].values()):
            copy.wait_send()


def settle(*refs):
    *ends, sem = refs
    n = len(ends) // 2
    copies = [pltpu.make_async_copy(ends[i], ends[n + i], sem.at[i]) for i in range(n)]
    for copy in copies:
        copy.start()
    for copy in copies:
        copy.wait()


def solution(mesh):
    nx, ny, ng = mesh.shape["gx"], mesh.shape["gy"], mesh.shape["goal"]

    def per_device(potential, cost, obstacle, density, destinations, group_ids):
        goals, height, width = potential.shape
        groups = density.shape[0]
        halves = width // LANES
        rows = height + 2 * PAD
        nz = ng // 2
        f32 = jnp.float32

        def vm(*shape, dtype=f32):
            return pltpu.VMEM(shape, dtype)

        panel = (rows, LANES)
        flat = (height, LANES)
        scratch = [
            vm(goals, halves, *panel), vm(goals, halves, *panel), vm(2, *panel), vm(2, *panel), vm(halves, *panel), vm(2, *panel),
            vm(halves, *flat), vm(halves, *flat, dtype=jnp.int32),
            vm(groups, halves, *panel), vm(2, *panel), vm(*flat), vm(*flat), vm(*panel), vm(*panel),
            vm(groups, halves, *flat), vm(groups, *flat), vm(groups, *flat),
            vm(2, nz, groups, height // (2 * nz), LANES), vm(groups, halves, *panel), vm(2, *panel),
            vm(*flat), vm(*flat), vm(*panel), vm(*panel),
            vm(groups, halves, *panel), vm(groups, halves, *panel), vm(2, *panel), vm(2, *panel),
            vm(groups, halves, *flat),
            pltpu.SMEM((goals,), jnp.int32), pltpu.SMEM((goals,), jnp.int32),
            vm(*flat), vm(*flat), vm(*panel), vm(*panel),
            pltpu.SemaphoreType.DMA((32,)),
            pltpu.SemaphoreType.DMA((88,)),
            pltpu.SemaphoreType.DMA((88,)),
        ]
        anywhere = pl.BlockSpec(memory_space=pltpu.HBM)
        results = pl.pallas_call(
            functools.partial(kernel, nx, ny, nz, goals, groups, height, width),
            out_shape=(
                vm(*potential.shape),
                vm(groups, 2, height, width),
                vm(*density.shape),
            ),
            in_specs=[anywhere] * 6,
            out_specs=(pl.BlockSpec(memory_space=pltpu.VMEM),) * 3,
            scratch_shapes=scratch,
            compiler_params=pltpu.CompilerParams(
                collective_id=0, has_side_effects=True, vmem_limit_bytes=VMEM_LIMIT
            ),
            name="crowd_step",
        )(potential, cost, obstacle, density, destinations, group_ids)
        return pl.pallas_call(
            settle,
            out_shape=tuple(jax.ShapeDtypeStruct(r.shape, f32) for r in results),
            in_specs=[pl.BlockSpec(memory_space=pltpu.VMEM)] * 3,
            out_specs=(pl.BlockSpec(memory_space=pltpu.HBM),) * 3,
            scratch_shapes=[pltpu.SemaphoreType.DMA((3,))],
            compiler_params=pltpu.CompilerParams(vmem_limit_bytes=1 << 20),
            name="settle",
        )(*results)

    in_specs = (
        P("goal", "gx", "gy"),
        P("gx", "gy"),
        P("gx", "gy"),
        P(None, "gx", "gy"),
        P("goal"),
        P("goal"),
    )
    out_specs = (P("goal", "gx", "gy"), P(None, None, "gx", "gy"), P(None, "gx", "gy"))
    return jax.shard_map(
        per_device, mesh=mesh, in_specs=in_specs, out_specs=out_specs, check_vma=False
    )
```

```python
import functools

import jax
import jax.numpy as jnp
import numpy as np
from jax import lax
from jax.experimental import pallas as pl
from jax.experimental.pallas import tpu as pltpu
from jax.sharding import PartitionSpec as P

MESH = pl.DeviceIdType.MESH
SWEEPS = 8
CELL_SIZE = 0.005
SWEEP_TEMP = 0.002
GOAL_TEMP = 0.01
OBSTACLE_COST = 8.0
COURANT = 0.4
FAR = 10000.0
SHUT = 1e30
ABSENT = 1e28

LANES = 128
PAD = 16
U_SWEEP, U_BUILD, U_FIN = 9, 3, 4
VMEM_LIMIT = 67043328 - (2 << 20) - (64 << 10)
K_SWEEP = float(1.0 / (SWEEP_TEMP * np.log(2.0)))
K_GOAL = float(1.0 / (GOAL_TEMP * np.log(2.0)))


def roll(x, shift):
    shift %= LANES
    return x if shift == 0 else pltpu.roll(x, shift, 1)


def soft_min(items, k, temp):
    least = functools.reduce(jnp.minimum, items)
    total = functools.reduce(jnp.add, [jnp.exp2((least - item) * k) for item in items])
    return least - temp * jnp.log(total)


def loop(start, stop, body, unroll=1):
    def step(i, carry):
        body(i)
        return carry

    lax.fori_loop(start, stop, step, 0, unroll=unroll)


def tile_at(row):
    return pl.ds(pl.multiple_of(row, 8), 8)


def kernel(
    nx, ny, nz, goals, groups, height, width,
    pot, cost, obst, dens, dest_in, gid_in,
    pot_out, vel_out, den_out,
    XA, XB, SA, SB, S, Ss, Cb, Ob, D, Ds, ML, MR, RL, RR,
    G, G2, H, R, F, Fs, FM, FR, Vx, Vy, Vxs, Vys, DO,
    dest, gid, DML, DMR, DRL, DRR, lsem, ssem, rsem,
):
    X, St = (XA, XB), (SA, SB)
    halves = width // LANES
    rows_all = height + 2 * PAD
    bottom = PAD + height
    ix, iy, ig = lax.axis_index("gx"), lax.axis_index("gy"), lax.axis_index("goal")
    z, core = ig // 2, ig % 2
    xs = {-1: lax.rem(ix + nx - 1, nx), 0: ix, 1: lax.rem(ix + 1, nx)}
    ys = {-1: lax.rem(iy + ny - 1, ny), 0: iy, 1: lax.rem(iy + 1, ny)}
    partner = (ix, iy, 2 * z + (1 - core))
    z_at = [lax.rem(z + d, nz) for d in range(nz)]
    z_back = [lax.rem(z + nz - d, nz) for d in range(nz)]
    z_peer = [(ix, iy, 2 * z_at[d] + core) for d in range(nz)]
    around = [(dx, dy) for dx in (-1, 0, 1) for dy in (-1, 0, 1) if (dx, dy) != (0, 0)]
    at_top, at_bottom = ix == 0, ix == nx - 1
    at_left, at_right = iy == 0, iy == ny - 1

    barrier = pltpu.get_barrier_semaphore()
    greet = [(xs[dx], ys[dy], 2 * z + c) for dx, dy in around for c in (0, 1)]
    greet += [partner] + z_peer[1:]
    for device in greet:
        pl.semaphore_signal(barrier, inc=1, device_id=device, device_id_type=MESH)

    count = [0]

    def local(src, dst):
        copy = pltpu.make_async_copy(src, dst, lsem.at[count[0]])
        count[0] += 1
        copy.start()
        return copy

    body_rows = pl.ds(PAD, height)
    first, last = pl.ds(0, 8), pl.ds(height - 8, 8)
    above, below = pl.ds(PAD - 8, 8), pl.ds(bottom, 8)
    p_first, p_last = pl.ds(PAD, 8), pl.ds(bottom - 8, 8)
    cut = [pl.ds(LANES * h, LANES) for h in range(halves)]

    cost_in = [local(cost.at[:, cut[h]], Cb.at[h]) for h in range(halves)]
    cost_in += [local(obst.at[:, cut[h]], Ob.at[h]) for h in range(halves)]
    field_in = [local(pot.at[:, :, cut[h]], XA.at[:, h, body_rows]) for h in range(halves)]
    scalars_in = [local(dest_in, dest), local(gid_in, gid)]
    density_in = [local(dens.at[:, :, cut[h]], D.at[:, h, body_rows]) for h in range(halves)]

    sent = [0]

    def remote(src, dst, device):
        copy = pltpu.make_async_remote_copy(
            src_ref=src, dst_ref=dst, send_sem=ssem.at[sent[0]], recv_sem=rsem.at[sent[0]],
            device_id=device, device_id_type=MESH,
        )
        sent[0] += 1
        copy.start()
        return copy

    pl.semaphore_wait(barrier, len(greet))
    north, south = (xs[-1], ys[0], ig), (xs[1], ys[0], ig)
    halo = []
    for h in range(halves):
        halo.append(remote(pot.at[:, first, cut[h]], XA.at[:, h, below], north))
        halo.append(remote(pot.at[:, last, cut[h]], XA.at[:, h, above], south))

    lane = lax.broadcasted_iota(jnp.int32, (8, LANES), 1)
    sub = lax.broadcasted_iota(jnp.int32, (8, LANES), 0)
    slot = lane // 32
    offset = lane % 32

    for buffer in (0, 1):
        for h in range(halves):
            for g in range(goals):
                X[buffer][g, h, 0:8] = jnp.zeros((8, LANES), jnp.float32)
                X[buffer][g, h, rows_all - 8 : rows_all] = jnp.zeros((8, LANES), jnp.float32)
            St[buffer][h, 0:8] = jnp.zeros((8, LANES), jnp.float32)
            St[buffer][h, rows_all - 8 : rows_all] = jnp.zeros((8, LANES), jnp.float32)

    for copy in cost_in:
        copy.wait()

    def make_cost(i):
        for h in range(halves):
            blocked = Ob[h, tile_at(8 * i)].astype(jnp.float32)
            S[h, tile_at(PAD + 8 * i)] = (Cb[h, tile_at(8 * i)] + OBSTACLE_COST * blocked) * CELL_SIZE

    loop(0, height // 8, make_cost, unroll=2)
    halo.append(remote(S.at[:, p_first], S.at[:, below], north))
    halo.append(remote(S.at[:, p_last], S.at[:, above], south))
    for copy in field_in:
        copy.wait()

    def in_slots(tiles, shift):
        out = roll(tiles[0], shift)
        for g in range(1, len(tiles)):
            out = jnp.where(slot == g, roll(tiles[g], shift + 32 * g), out)
        return out

    def repeated(tile, shift):
        out = jnp.where(offset < 8, roll(tile, shift), 0.0)
        return out

    right_edge = 8 - LANES

    def pack(i):
        t = tile_at(PAD + 8 * i)
        tm = tile_at(8 * i)
        p = [XA[g, halves - 1, t] for g in range(goals)]
        s = [S[halves - 1, t]] * goals
        MR[tm] = jnp.where(offset < 8, in_slots(p, right_edge), in_slots(s, right_edge + 8))
        p = [XA[g, 0, t] for g in range(goals)]
        s = [S[0, t]] * goals
        ML[tm] = jnp.where(offset >= 24, in_slots(p, 24), in_slots(s, 16))

    loop(0, height // 8, pack, unroll=4)

    def pack_columns(source, mr, ml):
        def one(i):
            t, tm = tile_at(PAD + 8 * i), tile_at(8 * i)
            mr[tm] = in_slots([source[k, halves - 1, t] for k in range(groups)], right_edge)
            ml[tm] = in_slots([source[k, 0, t] for k in range(groups)], 24)

        return one

    def send_sides(mr, ml, rl, rr, start, rows):
        here, there = pl.ds(start, rows), pl.ds(PAD + start, rows)
        return [
            remote(mr.at[here], rl.at[there], (xs[0], ys[1], ig)),
            remote(ml.at[here], rr.at[there], (xs[0], ys[-1], ig)),
        ]

    def send_corners(mr, ml, rl, rr, dx):
        here, there = (first, below) if dx < 0 else (last, above)
        return [
            remote(mr.at[here], rl.at[there], (xs[dx], ys[1], ig)),
            remote(ml.at[here], rr.at[there], (xs[dx], ys[-1], ig)),
        ]

    halo += send_sides(MR, ML, RL, RR, 0, height)
    halo += send_corners(MR, ML, RL, RR, -1) + send_corners(MR, ML, RL, RR, 1)
    late = []
    for h in range(halves):
        late.append(remote(dens.at[:, first, cut[h]], D.at[:, h, below], north))
        late.append(remote(dens.at[:, last, cut[h]], D.at[:, h, above], south))

    n_ext = height // 8 + 2
    own_left, own_right = offset >= 8, offset < 24

    def build_own(i):
        t = tile_at(PAD - 8 + 8 * i)
        SA[0, t] = in_slots([XA[g, 0, t] for g in range(goals)], 8)
        SA[1, t] = in_slots([XA[g, halves - 1, t] for g in range(goals)], 24 - LANES)

    def build(i):
        t = tile_at(PAD - 8 + 8 * i)
        from_left, from_right = RL[t], RR[t]
        s = jnp.where(own_left, in_slots([S[0, t]] * goals, 8), roll(from_left, -8))
        s_left = jnp.where(at_left & ~own_left, SHUT, s)
        p = jnp.where(own_left, SA[0, t], from_left)
        SA[0, t] = jnp.where(at_left & ~own_left, FAR - roll(s, -1), p)
        Ss[0, t] = s_left
        shift = 24 - LANES
        s = jnp.where(own_right, in_slots([S[halves - 1, t]] * goals, shift), roll(from_right, 8))
        s_right = jnp.where(at_right & ~own_right, SHUT, s)
        p = jnp.where(own_right, SA[1, t], from_right)
        SA[1, t] = jnp.where(at_right & ~own_right, FAR - roll(s, 1), p)
        Ss[1, t] = s_right

    for copy in scalars_in:
        copy.wait()
    width_all = width * ny
    cell = sub * width + lane
    target, strip_row = [], [jnp.full((8, LANES), -1000, jnp.int32) for _ in (0, 1)]
    for g in range(goals):
        row = dest[g] // width_all - ix * height
        col = dest[g] % width_all - iy * width
        held = (col >= 0) & (col < width)
        target.append(jnp.where(held, row * width + col, -(1 << 24)))
        for side, start in ((0, -8), (1, width - 24)):
            here = (slot == g) & (offset + start == col)
            strip_row[side] = jnp.where(here, row, strip_row[side])

    def relax(centre, up, down, left, right, s):
        beside = (up, down, left, right)
        near = jnp.minimum(jnp.minimum(up, down), jnp.minimum(left, right))
        least = jnp.minimum(centre, near + s)
        total = jnp.exp2((least - centre) * K_SWEEP)
        level = least - s
        for item in beside:
            total += jnp.exp2((level - item) * K_SWEEP)
        return least - SWEEP_TEMP * jnp.log(total)

    def three(base):
        return tile_at(base), pl.ds(base - 1, 8), pl.ds(base + 1, 8)

    def sweep(number, lo, hi, main, strips):
        now, later = (number - 1) % 2, number % 2

        def tile(i):
            t, tu, td = three(PAD - 8 + 8 * i)
            row = 8 * i - 8
            if main:
                s = [S[h, t] for h in range(halves)]
                for g in range(goals):
                    centre = [X[now][g, h, t] for h in range(halves)]
                    to_right = [roll(c, 1) for c in centre]
                    to_left = [roll(c, -1) for c in centre]
                    for h in range(halves):
                        left, right = to_right[h], to_left[h]
                        if h > 0:
                            left = jnp.where(lane == 0, to_right[h - 1], left)
                        if h < halves - 1:
                            right = jnp.where(lane == LANES - 1, to_left[h + 1], right)
                        new = relax(centre[h], X[now][g, h, tu], X[now][g, h, td], left, right, s[h])
                        pinned = cell == target[g] - (row * width + LANES * h)
                        X[later][g, h, t] = jnp.where(pinned, 0.0, new)
            if strips:
                for side in (0, 1):
                    c = St[now][side, t]
                    new = relax(
                        c, St[now][side, tu], St[now][side, td], roll(c, 1), roll(c, -1), Ss[side, t]
                    )
                    St[later][side, t] = jnp.where(strip_row[side] == sub + row, 0.0, new)

        if hi > lo:
            loop(lo, hi, tile, unroll=hi - lo)

    loop(1, n_ext - 1, build_own, unroll=4)
    early = 3
    for number in range(1, early + 1):
        sweep(number, number + 1, n_ext - 1 - number, True, False)
    for copy in halo:
        copy.wait()
    build_own(0)
    build_own(n_ext - 1)
    loop(0, n_ext, build, unroll=U_BUILD)

    for flag, ghost, inner in ((at_top, above, PAD), (at_bottom, below, bottom - 1)):
        for h in range(halves):
            beside = jnp.broadcast_to(FAR - S[h, inner : inner + 1], (8, LANES))
            for g in range(goals):
                XA[g, h, ghost] = jnp.where(flag, beside, XA[g, h, ghost])
            S[h, ghost] = jnp.where(flag, SHUT, S[h, ghost])
        for side in (0, 1):
            beside = Ss[side, inner : inner + 1]
            beside = jnp.where(beside < SHUT, FAR - beside, FAR)
            beside = jnp.broadcast_to(beside, (8, LANES))
            SA[side, ghost] = jnp.where(flag, beside, SA[side, ghost])
            Ss[side, ghost] = jnp.where(flag, SHUT, Ss[side, ghost])

    for number in range(1, SWEEPS + 1):
        start, stop = (1 if number == SWEEPS else 0), n_ext - 1 - number
        if number <= early:
            sweep(number, start, number + 1, True, True)
            sweep(number, number + 1, stop, False, True)
        else:
            sweep(number, start, stop, True, True)

    def lower(number):
        sweep(number, n_ext - 1 - number, n_ext - (1 if number == SWEEPS else 0), True, True)

    bias = [[jnp.where(gid[g] == k, 0.0, ABSENT) for k in range(groups)] for g in range(goals)]

    def merged(main, left, right, g, h):
        if h == 0:
            main = jnp.where(lane < 8, roll(left, -(32 * g + 8)), main)
        if h == halves - 1:
            main = jnp.where(lane >= LANES - 8, roll(right, LANES - 24 - 32 * g), main)
        return main

    def finish(i):
        t = tile_at(PAD + 8 * i)
        strips = [SA[side, t] for side in (0, 1)]
        for h in range(halves):
            p = [merged(XA[g, h, t], strips[0], strips[1], g, h) for g in range(goals)]
            for g in range(goals):
                pot_out[g, tile_at(8 * i), cut[h]] = p[g]
            for k in range(groups):
                G[k, h, tile_at(8 * i)] = soft_min(
                    [p[g] + bias[g][k] for g in range(goals)], K_GOAL, GOAL_TEMP
                )

    parts = 2
    part = height // parts
    tiles = part // 8
    swap, spread, gather, forward = [], [], [], []

    def part_rows(q):
        return pl.ds(part * q, part)

    def finish_part(q):
        piece = part // 2
        moves = []
        for start in (part * q, part * q + piece):
            loop(start // 8, (start + piece) // 8, finish, unroll=U_FIN)
            rows = pl.ds(start, piece)
            moves.append(remote(G.at[:, 1 - core, rows], G2.at[:, rows], partner))
        swap.append(moves)


    def join(i):
        t = tile_at(8 * i)
        for k in range(groups):
            H[k, t] = soft_min([G[k, core, t], G2[k, t]], K_GOAL, GOAL_TEMP)

    chunk = part // nz

    def block(q, j):
        return pl.ds(pl.multiple_of(part * q + chunk * j, 8), chunk)

    order = sorted(range(1, nz), key=lambda d: -min(d, nz - d))
    finish_part(0)
    for number in range(1, SWEEPS - 1):
        lower(number)
    for q in range(parts):
        for n, copy in enumerate(swap[q]):
            copy.wait_recv()
            loop(tiles * q + tiles // 2 * n, tiles * q + tiles // 2 * (n + 1), join, unroll=4)
        spread.append([remote(H.at[:, block(q, z_at[d])], R.at[q, d], z_peer[d]) for d in order])
        if q == 0:
            lower(SWEEPS - 1)
            lower(SWEEPS)
            finish_part(1)

    for copy in density_in:
        copy.wait()
    loop(0, height // 8, pack_columns(D, DMR, DML), unroll=4)
    late += send_sides(DMR, DML, DRL, DRR, 0, height)

    def mine(q, j):
        return F.at[:, core, pl.ds(pl.multiple_of(PAD + part * q + chunk * j, 8), chunk)]

    for q in range(parts):
        for copy in spread[q]:
            copy.wait_recv()
        for k in range(groups):
            for i in range(chunk // 8):
                row = part * q + chunk * z + 8 * i
                items = [H[k, tile_at(row)]]
                items += [R[q, d, k, 8 * i : 8 * i + 8] for d in range(1, nz)]
                F[k, core, tile_at(PAD + row)] = soft_min(items, K_GOAL, GOAL_TEMP)
        gather.append({d: remote(mine(q, z), mine(q, z), z_peer[d]) for d in order})
        forward.append(remote(mine(q, z), mine(q, z), partner))

    inv_two_cells = 1.0 / (2.0 * CELL_SIZE)

    def flow(up, down, left, right, speed):
        gx = (down - up) * inv_two_cells
        gy = (right - left) * inv_two_cells
        scale = speed * lax.rsqrt(1.0 + gx * gx + gy * gy)
        return -scale * gx, -scale * gy

    def sides(row, h):
        left, right = roll(row[h], 1), roll(row[h], -1)
        if h > 0:
            left = jnp.where(lane == 0, roll(row[h - 1], 1), left)
        if h < halves - 1:
            right = jnp.where(lane == LANES - 1, roll(row[h + 1], -1), right)
        return left, right

    def flows(i):
        t, tu, td = three(PAD - 8 + 8 * i)
        speed = []
        for h in range(halves):
            total = functools.reduce(jnp.add, [D[k, h, t] for k in range(groups)])
            speed.append(1.0 / (1.0 + total))
        for k in range(groups):
            centre = [F[k, h, t] for h in range(halves)]
            for h in range(halves):
                left, right = sides(centre, h)
                Vx[k, h, t], Vy[k, h, t] = flow(F[k, h, tu], F[k, h, td], left, right, speed[h])

    def strip_flows(i):
        t, tu, td = three(PAD - 8 + 8 * i)
        for side in (0, 1):
            d = Ds[side, t]
            d = d + roll(d, 32)
            d = d + roll(d, 64)
            c = Fs[side, t]
            Vxs[side, t], Vys[side, t] = flow(
                Fs[side, tu], Fs[side, td], roll(c, 1), roll(c, -1), 1.0 / (1.0 + d)
            )

    def flux(low_v, high_v, low_d, high_d):
        face = 0.5 * (low_v + high_v)
        return jnp.maximum(face, 0.0) * low_d + jnp.minimum(face, 0.0) * high_d

    def updated(i, vx, vxu, vxd, vy, vyl, vyr, d, du, dd, dl, dr, no_left, no_right):
        row = sub + 8 * i
        up = jnp.where(at_top & (row == 0), 0.0, flux(vxu, vx, du, d))
        down = jnp.where(at_bottom & (row == height - 1), 0.0, flux(vx, vxd, d, dd))
        left, right = flux(vyl, vy, dl, d), flux(vy, vyr, d, dr)
        left = left if no_left is None else jnp.where(no_left, 0.0, left)
        right = right if no_right is None else jnp.where(no_right, 0.0, right)
        return d - COURANT * (down - up + right - left)

    def advect(i):
        t, tu, td = three(PAD + 8 * i)
        for k in range(groups):
            vy = [Vy[k, h, t] for h in range(halves)]
            d = [D[k, h, t] for h in range(halves)]
            for h in range(halves):
                vyl, vyr = sides(vy, h)
                dl, dr = sides(d, h)
                DO[k, h, tile_at(8 * i)] = updated(
                    i, Vx[k, h, t], Vx[k, h, tu], Vx[k, h, td], vy[h], vyl, vyr,
                    d[h], D[k, h, tu], D[k, h, td], dl, dr, None, None,
                )

    def strip_advect(i):
        t, tu, td = three(PAD + 8 * i)
        to = tile_at(8 * i)
        strips = []
        for side in (0, 1):
            vx, vy, d = Vxs[side, t], Vys[side, t], Ds[side, t]
            new = updated(
                i, vx, Vxs[side, tu], Vxs[side, td], vy, roll(vy, 1), roll(vy, -1),
                d, Ds[side, tu], Ds[side, td], roll(d, 1), roll(d, -1),
                (at_left & (offset == 8)) if side == 0 else None,
                (at_right & (offset == 23)) if side == 1 else None,
            )
            strips.append((vx, vy, new))
        for k in range(groups):
            for h in range(halves):
                vel_out[k, 0, to, cut[h]] = merged(Vx[k, h, t], strips[0][0], strips[1][0], k, h)
                vel_out[k, 1, to, cut[h]] = merged(Vy[k, h, t], strips[0][1], strips[1][1], k, h)
                den_out[k, to, cut[h]] = merged(DO[k, h, to], strips[0][2], strips[1][2], k, h)

    def build_density(i):
        t = tile_at(PAD - 8 + 8 * i)
        own = in_slots([D[k, 0, t] for k in range(groups)], 8)
        Ds[0, t] = jnp.where(own_left, own, DRL[t])
        own = in_slots([D[k, halves - 1, t] for k in range(groups)], 24 - LANES)
        Ds[1, t] = jnp.where(own_right, own, DRR[t])

    def build_field(i):
        t = tile_at(PAD - 8 + 8 * i)
        f = jnp.where(own_left, in_slots([F[k, 0, t] for k in range(groups)], 8), FR[0, t])
        Fs[0, t] = jnp.where(at_left & ~own_left, roll(f, -1), f)
        f = jnp.where(
            own_right, in_slots([F[k, halves - 1, t] for k in range(groups)], 24 - LANES), FR[1, t]
        )
        Fs[1, t] = jnp.where(at_right & ~own_right, roll(f, 1), f)

    toward = lax.rem(iy + ny - 1 + 2 * core, ny)
    shift = 24 - 16 * core

    def pack_field(i):
        t = tile_at(PAD + 8 * i)
        out = pltpu.roll(F[0, core, t], shift, 1)
        for k in range(1, groups):
            out = jnp.where(slot == k, pltpu.roll(F[k, core, t], shift + 32 * k, 1), out)
        FM[tile_at(8 * i)] = out

    class Both:
        def __init__(self, src, dst_of, x, y):
            base = sent[0]
            sent[0] += 2
            self.sends, self.receipts = [], []
            for c in (0, 1):
                copy = pltpu.make_async_remote_copy(
                    src_ref=src, dst_ref=dst_of(core),
                    send_sem=ssem.at[base + c], recv_sem=rsem.at[base + core],
                    device_id=(x, y, 2 * z + c), device_id_type=MESH,
                )
                copy.start()
                self.sends.append(copy)
                self.receipts.append(
                    pltpu.make_async_remote_copy(
                        src_ref=src, dst_ref=dst_of(c),
                        send_sem=ssem.at[base + c], recv_sem=rsem.at[base + c],
                        device_id=(x, y, 2 * z + c), device_id_type=MESH,
                    )
                )

        def wait(self):
            for copy in self.receipts:
                copy.wait_recv()
            for copy in self.sends:
                copy.wait_send()

    def columns(rows):
        return lambda c: FR.at[1 - c, rows]

    halos = []

    def collect(q):
        arrived = []
        for d in order[::-1]:
            gather[q][d].wait_recv()
            arrived.append(remote(mine(q, z_back[d]), mine(q, z_back[d]), partner))
        dx, here, there, row = ((-1, first, below, p_first), (1, last, above, p_last))[q]
        loop(tiles * q, tiles * (q + 1), pack_field, unroll=4)
        side = pl.ds(part * q, part), pl.ds(PAD + part * q, part)
        out = [Both(FM.at[side[0]], columns(side[1]), ix, toward)]
        out.append(Both(FM.at[here], columns(there), xs[dx], toward))
        out.append(Both(F.at[:, core, row], lambda c: F.at[:, c, there], xs[dx], iy))
        halos.append(out)
        for copy in [forward[q]] + arrived:
            copy.wait_recv()
        return arrived

    passed = collect(0)
    loop(2, 8, flows, unroll=2)
    loop(2, 6, advect, unroll=2)
    passed += collect(1)
    loop(8, n_ext - 2, flows, unroll=2)
    loop(6, height // 8 - 2, advect, unroll=2)
    for copy in late:
        copy.wait()
    loop(0, n_ext, build_density, unroll=6)
    for copy in halos[0]:
        copy.wait()
    loop(1, 9, build_field, unroll=4)
    loop(2, 8, strip_flows, unroll=6)
    loop(2, 6, strip_advect, unroll=2)
    for copy in halos[1]:
        copy.wait()

    for flag, ghost, inner in ((at_top, above, PAD), (at_bottom, below, bottom - 1)):
        for h in range(halves):
            for k in range(groups):
                beside = jnp.broadcast_to(F[k, h, inner : inner + 1], (8, LANES))
                F[k, h, ghost] = jnp.where(flag, beside, F[k, h, ghost])
    build_field(0)
    loop(9, n_ext, build_field, unroll=9)
    for flag, ghost, inner in ((at_top, above, PAD), (at_bottom, below, bottom - 1)):
        for side in (0, 1):
            beside = jnp.broadcast_to(Fs[side, inner : inner + 1], (8, LANES))
            Fs[side, ghost] = jnp.where(flag, beside, Fs[side, ghost])
    for i in (0, 1, n_ext - 2, n_ext - 1):
        flows(i)
    for i in (0, 1):
        strip_flows(i)
    loop(8, n_ext, strip_flows, unroll=10)
    for i in (0, 1, height // 8 - 2, height // 8 - 1):
        advect(i)
    loop(0, 2, strip_advect, unroll=2)
    loop(6, height // 8, strip_advect, unroll=2)

    for copy in swap[0] + swap[1] + forward + passed:
        copy.wait_send()
    for q in range(parts):
        for copy in spread[q] + list(gather[q].values()):
            copy.wait_send()


def settle(*refs):
    *ends, sem = refs
    n = len(ends) // 2
    copies = [pltpu.make_async_copy(ends[i], ends[n + i], sem.at[i]) for i in range(n)]
    for copy in copies:
        copy.start()
    for copy in copies:
        copy.wait()


def solution(mesh):
    nx, ny, ng = mesh.shape["gx"], mesh.shape["gy"], mesh.shape["goal"]

    def per_device(potential, cost, obstacle, density, destinations, group_ids):
        goals, height, width = potential.shape
        groups = density.shape[0]
        halves = width // LANES
        rows = height + 2 * PAD
        nz = ng // 2
        f32 = jnp.float32

        def vm(*shape, dtype=f32):
            return pltpu.VMEM(shape, dtype)

        panel = (rows, LANES)
        flat = (height, LANES)
        scratch = [
            vm(goals, halves, *panel), vm(goals, halves, *panel), vm(2, *panel), vm(2, *panel), vm(halves, *panel), vm(2, *panel),
            vm(halves, *flat), vm(halves, *flat, dtype=jnp.int32),
            vm(groups, halves, *panel), vm(2, *panel), vm(*flat), vm(*flat), vm(*panel), vm(*panel),
            vm(groups, halves, *flat), vm(groups, *flat), vm(groups, *flat),
            vm(2, nz, groups, height // (2 * nz), LANES), vm(groups, halves, *panel), vm(2, *panel),
            vm(*flat), vm(2, *panel),
            vm(groups, halves, *panel), vm(groups, halves, *panel), vm(2, *panel), vm(2, *panel),
            vm(groups, halves, *flat),
            pltpu.SMEM((goals,), jnp.int32), pltpu.SMEM((goals,), jnp.int32),
            vm(*flat), vm(*flat), vm(*panel), vm(*panel),
            pltpu.SemaphoreType.DMA((32,)),
            pltpu.SemaphoreType.DMA((88,)),
            pltpu.SemaphoreType.DMA((88,)),
        ]
        anywhere = pl.BlockSpec(memory_space=pltpu.HBM)
        results = pl.pallas_call(
            functools.partial(kernel, nx, ny, nz, goals, groups, height, width),
            out_shape=(
                vm(*potential.shape),
                vm(groups, 2, height, width),
                vm(*density.shape),
            ),
            in_specs=[anywhere] * 6,
            out_specs=(pl.BlockSpec(memory_space=pltpu.VMEM),) * 3,
            scratch_shapes=scratch,
            compiler_params=pltpu.CompilerParams(
                collective_id=0, has_side_effects=True, vmem_limit_bytes=VMEM_LIMIT
            ),
            name="crowd_step",
        )(potential, cost, obstacle, density, destinations, group_ids)
        return pl.pallas_call(
            settle,
            out_shape=tuple(jax.ShapeDtypeStruct(r.shape, f32) for r in results),
            in_specs=[pl.BlockSpec(memory_space=pltpu.VMEM)] * 3,
            out_specs=(pl.BlockSpec(memory_space=pltpu.HBM),) * 3,
            scratch_shapes=[pltpu.SemaphoreType.DMA((3,))],
            compiler_params=pltpu.CompilerParams(vmem_limit_bytes=1 << 20),
            name="settle",
        )(*results)

    in_specs = (
        P("goal", "gx", "gy"),
        P("gx", "gy"),
        P("gx", "gy"),
        P(None, "gx", "gy"),
        P("goal"),
        P("goal"),
    )
    out_specs = (P("goal", "gx", "gy"), P(None, None, "gx", "gy"), P(None, "gx", "gy"))
    return jax.shard_map(
        per_device, mesh=mesh, in_specs=in_specs, out_specs=out_specs, check_vma=False
    )
```

```python
import functools

import jax
import jax.numpy as jnp
import numpy as np
from jax import lax
from jax.experimental import pallas as pl
from jax.experimental.pallas import tpu as pltpu
from jax.sharding import PartitionSpec as P

MESH = pl.DeviceIdType.MESH
SWEEPS = 8
CELL_SIZE = 0.005
SWEEP_TEMP = 0.002
GOAL_TEMP = 0.01
OBSTACLE_COST = 8.0
COURANT = 0.4
FAR = 10000.0
SHUT = 1e30
ABSENT = 1e28

LANES = 128
PAD = 16
U_SWEEP, U_BUILD, U_FIN = 9, 3, 4
VMEM_LIMIT = 67043328 - (2 << 20) - (64 << 10)
K_SWEEP = float(1.0 / (SWEEP_TEMP * np.log(2.0)))
K_GOAL = float(1.0 / (GOAL_TEMP * np.log(2.0)))


def roll(x, shift):
    shift %= LANES
    return x if shift == 0 else pltpu.roll(x, shift, 1)


def soft_min(items, k, temp):
    least = functools.reduce(jnp.minimum, items)
    total = functools.reduce(jnp.add, [jnp.exp2((least - item) * k) for item in items])
    return least - temp * jnp.log(total)


def loop(start, stop, body, unroll=1):
    def step(i, carry):
        body(i)
        return carry

    lax.fori_loop(start, stop, step, 0, unroll=unroll)


def tile_at(row):
    return pl.ds(pl.multiple_of(row, 8), 8)


def kernel(
    nx, ny, nz, goals, groups, height, width,
    pot, cost, obst, dens, dest_in, gid_in,
    pot_out, vel_out, den_out,
    XA, XB, SA, SB, S, Ss, Cb, Ob, D, Ds, ML, MR, RL, RR,
    G, G2, H, R, F, Fs, FM, FR, Vx, Vy, Vxs, Vys, DO,
    dest, gid, DML, DMR, DRL, DRR, lsem, ssem, rsem,
):
    X, St = (XA, XB), (SA, SB)
    halves = width // LANES
    rows_all = height + 2 * PAD
    bottom = PAD + height
    ix, iy, ig = lax.axis_index("gx"), lax.axis_index("gy"), lax.axis_index("goal")
    z, core = ig // 2, ig % 2
    xs = {-1: lax.rem(ix + nx - 1, nx), 0: ix, 1: lax.rem(ix + 1, nx)}
    ys = {-1: lax.rem(iy + ny - 1, ny), 0: iy, 1: lax.rem(iy + 1, ny)}
    partner = (ix, iy, 2 * z + (1 - core))
    z_at = [lax.rem(z + d, nz) for d in range(nz)]
    z_back = [lax.rem(z + nz - d, nz) for d in range(nz)]
    z_peer = [(ix, iy, 2 * z_at[d] + core) for d in range(nz)]
    around = [(dx, dy) for dx in (-1, 0, 1) for dy in (-1, 0, 1) if (dx, dy) != (0, 0)]
    at_top, at_bottom = ix == 0, ix == nx - 1
    at_left, at_right = iy == 0, iy == ny - 1

    barrier = pltpu.get_barrier_semaphore()
    greet = [(xs[dx], ys[dy], 2 * z + c) for dx, dy in around for c in (0, 1)]
    greet += [partner] + z_peer[1:]
    for device in greet:
        pl.semaphore_signal(barrier, inc=1, device_id=device, device_id_type=MESH)

    count = [0]

    def local(src, dst):
        copy = pltpu.make_async_copy(src, dst, lsem.at[count[0]])
        count[0] += 1
        copy.start()
        return copy

    body_rows = pl.ds(PAD, height)
    first, last = pl.ds(0, 8), pl.ds(height - 8, 8)
    above, below = pl.ds(PAD - 8, 8), pl.ds(bottom, 8)
    p_first, p_last = pl.ds(PAD, 8), pl.ds(bottom - 8, 8)
    cut = [pl.ds(LANES * h, LANES) for h in range(halves)]

    cost_in = [local(cost.at[:, cut[h]], Cb.at[h]) for h in range(halves)]
    cost_in += [local(obst.at[:, cut[h]], Ob.at[h]) for h in range(halves)]
    field_in = [local(pot.at[:, :, cut[h]], XA.at[:, h, body_rows]) for h in range(halves)]
    scalars_in = [local(dest_in, dest), local(gid_in, gid)]
    density_in = [local(dens.at[:, :, cut[h]], D.at[:, h, body_rows]) for h in range(halves)]

    sent = [0]

    def remote(src, dst, device):
        copy = pltpu.make_async_remote_copy(
            src_ref=src, dst_ref=dst, send_sem=ssem.at[sent[0]], recv_sem=rsem.at[sent[0]],
            device_id=device, device_id_type=MESH,
        )
        sent[0] += 1
        copy.start()
        return copy

    pl.semaphore_wait(barrier, len(greet))
    north, south = (xs[-1], ys[0], ig), (xs[1], ys[0], ig)
    halo = []
    for h in range(halves):
        halo.append(remote(pot.at[:, first, cut[h]], XA.at[:, h, below], north))
        halo.append(remote(pot.at[:, last, cut[h]], XA.at[:, h, above], south))

    lane = lax.broadcasted_iota(jnp.int32, (8, LANES), 1)
    sub = lax.broadcasted_iota(jnp.int32, (8, LANES), 0)
    slot = lane // 32
    offset = lane % 32

    for buffer in (0, 1):
        for h in range(halves):
            for g in range(goals):
                X[buffer][g, h, 0:8] = jnp.zeros((8, LANES), jnp.float32)
                X[buffer][g, h, rows_all - 8 : rows_all] = jnp.zeros((8, LANES), jnp.float32)
            St[buffer][h, 0:8] = jnp.zeros((8, LANES), jnp.float32)
            St[buffer][h, rows_all - 8 : rows_all] = jnp.zeros((8, LANES), jnp.float32)

    for copy in cost_in:
        copy.wait()

    def make_cost(i):
        for h in range(halves):
            blocked = Ob[h, tile_at(8 * i)].astype(jnp.float32)
            S[h, tile_at(PAD + 8 * i)] = (Cb[h, tile_at(8 * i)] + OBSTACLE_COST * blocked) * CELL_SIZE

    loop(0, height // 8, make_cost, unroll=2)
    halo.append(remote(S.at[:, p_first], S.at[:, below], north))
    halo.append(remote(S.at[:, p_last], S.at[:, above], south))
    for copy in field_in:
        copy.wait()

    def in_slots(tiles, shift):
        out = roll(tiles[0], shift)
        for g in range(1, len(tiles)):
            out = jnp.where(slot == g, roll(tiles[g], shift + 32 * g), out)
        return out

    def repeated(tile, shift):
        out = jnp.where(offset < 8, roll(tile, shift), 0.0)
        return out

    right_edge = 8 - LANES

    def pack(i):
        t = tile_at(PAD + 8 * i)
        tm = tile_at(8 * i)
        p = [XA[g, halves - 1, t] for g in range(goals)]
        s = [S[halves - 1, t]] * goals
        MR[tm] = jnp.where(offset < 8, in_slots(p, right_edge), in_slots(s, right_edge + 8))
        p = [XA[g, 0, t] for g in range(goals)]
        s = [S[0, t]] * goals
        ML[tm] = jnp.where(offset >= 24, in_slots(p, 24), in_slots(s, 16))

    loop(0, height // 8, pack, unroll=4)

    def pack_columns(source, mr, ml):
        def one(i):
            t, tm = tile_at(PAD + 8 * i), tile_at(8 * i)
            mr[tm] = in_slots([source[k, halves - 1, t] for k in range(groups)], right_edge)
            ml[tm] = in_slots([source[k, 0, t] for k in range(groups)], 24)

        return one

    def send_sides(mr, ml, rl, rr, start, rows):
        here, there = pl.ds(start, rows), pl.ds(PAD + start, rows)
        return [
            remote(mr.at[here], rl.at[there], (xs[0], ys[1], ig)),
            remote(ml.at[here], rr.at[there], (xs[0], ys[-1], ig)),
        ]

    def send_corners(mr, ml, rl, rr, dx):
        here, there = (first, below) if dx < 0 else (last, above)
        return [
            remote(mr.at[here], rl.at[there], (xs[dx], ys[1], ig)),
            remote(ml.at[here], rr.at[there], (xs[dx], ys[-1], ig)),
        ]

    halo += send_sides(MR, ML, RL, RR, 0, height)
    halo += send_corners(MR, ML, RL, RR, -1) + send_corners(MR, ML, RL, RR, 1)
    late = []
    for h in range(halves):
        late.append(remote(dens.at[:, first, cut[h]], D.at[:, h, below], north))
        late.append(remote(dens.at[:, last, cut[h]], D.at[:, h, above], south))

    n_ext = height // 8 + 2
    own_left, own_right = offset >= 8, offset < 24

    def build_own(i):
        t = tile_at(PAD - 8 + 8 * i)
        SA[0, t] = in_slots([XA[g, 0, t] for g in range(goals)], 8)
        SA[1, t] = in_slots([XA[g, halves - 1, t] for g in range(goals)], 24 - LANES)

    def build(i):
        t = tile_at(PAD - 8 + 8 * i)
        from_left, from_right = RL[t], RR[t]
        s = jnp.where(own_left, in_slots([S[0, t]] * goals, 8), roll(from_left, -8))
        s_left = jnp.where(at_left & ~own_left, SHUT, s)
        p = jnp.where(own_left, SA[0, t], from_left)
        SA[0, t] = jnp.where(at_left & ~own_left, FAR - roll(s, -1), p)
        Ss[0, t] = s_left
        shift = 24 - LANES
        s = jnp.where(own_right, in_slots([S[halves - 1, t]] * goals, shift), roll(from_right, 8))
        s_right = jnp.where(at_right & ~own_right, SHUT, s)
        p = jnp.where(own_right, SA[1, t], from_right)
        SA[1, t] = jnp.where(at_right & ~own_right, FAR - roll(s, 1), p)
        Ss[1, t] = s_right

    for copy in scalars_in:
        copy.wait()
    width_all = width * ny
    cell = sub * width + lane
    target, strip_row = [], [jnp.full((8, LANES), -1000, jnp.int32) for _ in (0, 1)]
    for g in range(goals):
        row = dest[g] // width_all - ix * height
        col = dest[g] % width_all - iy * width
        held = (col >= 0) & (col < width)
        target.append(jnp.where(held, row * width + col, -(1 << 24)))
        for side, start in ((0, -8), (1, width - 24)):
            here = (slot == g) & (offset + start == col)
            strip_row[side] = jnp.where(here, row, strip_row[side])

    def relax(centre, up, down, left, right, s):
        beside = (up, down, left, right)
        near = jnp.minimum(jnp.minimum(up, down), jnp.minimum(left, right))
        least = jnp.minimum(centre, near + s)
        total = jnp.exp2((least - centre) * K_SWEEP)
        level = least - s
        for item in beside:
            total += jnp.exp2((level - item) * K_SWEEP)
        return least - SWEEP_TEMP * jnp.log(total)

    def three(base):
        return tile_at(base), pl.ds(base - 1, 8), pl.ds(base + 1, 8)

    def sweep(number, lo, hi, main, strips):
        now, later = (number - 1) % 2, number % 2

        def tile(i):
            t, tu, td = three(PAD - 8 + 8 * i)
            row = 8 * i - 8
            if main:
                s = [S[h, t] for h in range(halves)]
                for g in range(goals):
                    centre = [X[now][g, h, t] for h in range(halves)]
                    to_right = [roll(c, 1) for c in centre]
                    to_left = [roll(c, -1) for c in centre]
                    for h in range(halves):
                        left, right = to_right[h], to_left[h]
                        if h > 0:
                            left = jnp.where(lane == 0, to_right[h - 1], left)
                        if h < halves - 1:
                            right = jnp.where(lane == LANES - 1, to_left[h + 1], right)
                        new = relax(centre[h], X[now][g, h, tu], X[now][g, h, td], left, right, s[h])
                        pinned = cell == target[g] - (row * width + LANES * h)
                        X[later][g, h, t] = jnp.where(pinned, 0.0, new)
            if strips:
                for side in (0, 1):
                    c = St[now][side, t]
                    new = relax(
                        c, St[now][side, tu], St[now][side, td], roll(c, 1), roll(c, -1), Ss[side, t]
                    )
                    St[later][side, t] = jnp.where(strip_row[side] == sub + row, 0.0, new)

        if hi > lo:
            loop(lo, hi, tile, unroll=hi - lo)

    loop(1, n_ext - 1, build_own, unroll=4)
    early = 3
    for number in range(1, early + 1):
        sweep(number, number + 1, n_ext - 1 - number, True, False)
    for copy in halo:
        copy.wait()
    build_own(0)
    build_own(n_ext - 1)
    loop(0, n_ext, build, unroll=U_BUILD)

    for flag, ghost, inner in ((at_top, above, PAD), (at_bottom, below, bottom - 1)):
        for h in range(halves):
            beside = jnp.broadcast_to(FAR - S[h, inner : inner + 1], (8, LANES))
            for g in range(goals):
                XA[g, h, ghost] = jnp.where(flag, beside, XA[g, h, ghost])
            S[h, ghost] = jnp.where(flag, SHUT, S[h, ghost])
        for side in (0, 1):
            beside = Ss[side, inner : inner + 1]
            beside = jnp.where(beside < SHUT, FAR - beside, FAR)
            beside = jnp.broadcast_to(beside, (8, LANES))
            SA[side, ghost] = jnp.where(flag, beside, SA[side, ghost])
            Ss[side, ghost] = jnp.where(flag, SHUT, Ss[side, ghost])

    for number in range(1, SWEEPS + 1):
        start, stop = (1 if number == SWEEPS else 0), n_ext - 1 - number
        if number <= early:
            sweep(number, start, number + 1, True, True)
            sweep(number, number + 1, stop, False, True)
        else:
            sweep(number, start, stop, True, True)

    def lower(number):
        sweep(number, n_ext - 1 - number, n_ext - (1 if number == SWEEPS else 0), True, True)

    bias = [[jnp.where(gid[g] == k, 0.0, ABSENT) for k in range(groups)] for g in range(goals)]

    def merged(main, left, right, g, h):
        if h == 0:
            main = jnp.where(lane < 8, roll(left, -(32 * g + 8)), main)
        if h == halves - 1:
            main = jnp.where(lane >= LANES - 8, roll(right, LANES - 24 - 32 * g), main)
        return main

    def finish(i):
        t = tile_at(PAD + 8 * i)
        strips = [SA[side, t] for side in (0, 1)]
        for h in range(halves):
            p = [merged(XA[g, h, t], strips[0], strips[1], g, h) for g in range(goals)]
            for g in range(goals):
                pot_out[g, tile_at(8 * i), cut[h]] = p[g]
            for k in range(groups):
                G[k, h, tile_at(8 * i)] = soft_min(
                    [p[g] + bias[g][k] for g in range(goals)], K_GOAL, GOAL_TEMP
                )

    parts = 2
    part = height // parts
    tiles = part // 8
    swap, spread, gather, forward = [], [], [], []

    def part_rows(q):
        return pl.ds(part * q, part)

    def finish_part(q):
        piece = part // 2
        moves = []
        for start in (part * q, part * q + piece):
            loop(start // 8, (start + piece) // 8, finish, unroll=U_FIN)
            rows = pl.ds(start, piece)
            moves.append(remote(G.at[:, 1 - core, rows], G2.at[:, rows], partner))
        swap.append(moves)


    def join(i):
        t = tile_at(8 * i)
        for k in range(groups):
            H[k, t] = soft_min([G[k, core, t], G2[k, t]], K_GOAL, GOAL_TEMP)

    chunk = part // nz

    def block(q, j):
        return pl.ds(pl.multiple_of(part * q + chunk * j, 8), chunk)

    order = sorted(range(1, nz), key=lambda d: -min(d, nz - d))
    finish_part(0)
    for number in range(1, SWEEPS - 1):
        lower(number)
    for q in range(parts):
        for n, copy in enumerate(swap[q]):
            copy.wait_recv()
            loop(tiles * q + tiles // 2 * n, tiles * q + tiles // 2 * (n + 1), join, unroll=4)
        spread.append([remote(H.at[:, block(q, z_at[d])], R.at[q, d], z_peer[d]) for d in order])
        if q == 0:
            lower(SWEEPS - 1)
            lower(SWEEPS)
            finish_part(1)

    for copy in density_in:
        copy.wait()
    loop(0, height // 8, pack_columns(D, DMR, DML), unroll=4)
    late += send_sides(DMR, DML, DRL, DRR, 0, height)

    def mine(q, j):
        return F.at[:, core, pl.ds(pl.multiple_of(PAD + part * q + chunk * j, 8), chunk)]

    near = [2, nz - 2, 1, nz - 1] if nz == 8 else order
    for q in range(parts):
        for copy in spread[q]:
            copy.wait_recv()
        for k in range(groups):
            for i in range(chunk // 8):
                row = part * q + chunk * z + 8 * i
                items = [H[k, tile_at(row)]]
                items += [R[q, d, k, 8 * i : 8 * i + 8] for d in range(1, nz)]
                F[k, core, tile_at(PAD + row)] = soft_min(items, K_GOAL, GOAL_TEMP)
        reach = near if q == 0 else order
        gather.append({d: remote(mine(q, z), mine(q, z), z_peer[d]) for d in reach})
        forward.append(remote(mine(q, z), mine(q, z), partner))

    inv_two_cells = 1.0 / (2.0 * CELL_SIZE)

    def flow(up, down, left, right, speed):
        gx = (down - up) * inv_two_cells
        gy = (right - left) * inv_two_cells
        scale = speed * lax.rsqrt(1.0 + gx * gx + gy * gy)
        return -scale * gx, -scale * gy

    def sides(row, h):
        left, right = roll(row[h], 1), roll(row[h], -1)
        if h > 0:
            left = jnp.where(lane == 0, roll(row[h - 1], 1), left)
        if h < halves - 1:
            right = jnp.where(lane == LANES - 1, roll(row[h + 1], -1), right)
        return left, right

    def flows(i):
        t, tu, td = three(PAD - 8 + 8 * i)
        speed = []
        for h in range(halves):
            total = functools.reduce(jnp.add, [D[k, h, t] for k in range(groups)])
            speed.append(1.0 / (1.0 + total))
        for k in range(groups):
            centre = [F[k, h, t] for h in range(halves)]
            for h in range(halves):
                left, right = sides(centre, h)
                Vx[k, h, t], Vy[k, h, t] = flow(F[k, h, tu], F[k, h, td], left, right, speed[h])

    def strip_flows(i):
        t, tu, td = three(PAD - 8 + 8 * i)
        for side in (0, 1):
            d = Ds[side, t]
            d = d + roll(d, 32)
            d = d + roll(d, 64)
            c = Fs[side, t]
            Vxs[side, t], Vys[side, t] = flow(
                Fs[side, tu], Fs[side, td], roll(c, 1), roll(c, -1), 1.0 / (1.0 + d)
            )

    def flux(low_v, high_v, low_d, high_d):
        face = 0.5 * (low_v + high_v)
        return jnp.maximum(face, 0.0) * low_d + jnp.minimum(face, 0.0) * high_d

    def updated(i, vx, vxu, vxd, vy, vyl, vyr, d, du, dd, dl, dr, no_left, no_right):
        row = sub + 8 * i
        up = jnp.where(at_top & (row == 0), 0.0, flux(vxu, vx, du, d))
        down = jnp.where(at_bottom & (row == height - 1), 0.0, flux(vx, vxd, d, dd))
        left, right = flux(vyl, vy, dl, d), flux(vy, vyr, d, dr)
        left = left if no_left is None else jnp.where(no_left, 0.0, left)
        right = right if no_right is None else jnp.where(no_right, 0.0, right)
        return d - COURANT * (down - up + right - left)

    def advect(i):
        t, tu, td = three(PAD + 8 * i)
        for k in range(groups):
            vy = [Vy[k, h, t] for h in range(halves)]
            d = [D[k, h, t] for h in range(halves)]
            for h in range(halves):
                vyl, vyr = sides(vy, h)
                dl, dr = sides(d, h)
                DO[k, h, tile_at(8 * i)] = updated(
                    i, Vx[k, h, t], Vx[k, h, tu], Vx[k, h, td], vy[h], vyl, vyr,
                    d[h], D[k, h, tu], D[k, h, td], dl, dr, None, None,
                )

    def strip_advect(i):
        t, tu, td = three(PAD + 8 * i)
        to = tile_at(8 * i)
        strips = []
        for side in (0, 1):
            vx, vy, d = Vxs[side, t], Vys[side, t], Ds[side, t]
            new = updated(
                i, vx, Vxs[side, tu], Vxs[side, td], vy, roll(vy, 1), roll(vy, -1),
                d, Ds[side, tu], Ds[side, td], roll(d, 1), roll(d, -1),
                (at_left & (offset == 8)) if side == 0 else None,
                (at_right & (offset == 23)) if side == 1 else None,
            )
            strips.append((vx, vy, new))
        for k in range(groups):
            for h in range(halves):
                vel_out[k, 0, to, cut[h]] = merged(Vx[k, h, t], strips[0][0], strips[1][0], k, h)
                vel_out[k, 1, to, cut[h]] = merged(Vy[k, h, t], strips[0][1], strips[1][1], k, h)
                den_out[k, to, cut[h]] = merged(DO[k, h, to], strips[0][2], strips[1][2], k, h)

    def build_density(i):
        t = tile_at(PAD - 8 + 8 * i)
        own = in_slots([D[k, 0, t] for k in range(groups)], 8)
        Ds[0, t] = jnp.where(own_left, own, DRL[t])
        own = in_slots([D[k, halves - 1, t] for k in range(groups)], 24 - LANES)
        Ds[1, t] = jnp.where(own_right, own, DRR[t])

    def build_field(i):
        t = tile_at(PAD - 8 + 8 * i)
        f = jnp.where(own_left, in_slots([F[k, 0, t] for k in range(groups)], 8), FR[0, t])
        Fs[0, t] = jnp.where(at_left & ~own_left, roll(f, -1), f)
        f = jnp.where(
            own_right, in_slots([F[k, halves - 1, t] for k in range(groups)], 24 - LANES), FR[1, t]
        )
        Fs[1, t] = jnp.where(at_right & ~own_right, roll(f, 1), f)

    toward = lax.rem(iy + ny - 1 + 2 * core, ny)
    shift = 24 - 16 * core

    def pack_field(i):
        t = tile_at(PAD + 8 * i)
        out = pltpu.roll(F[0, core, t], shift, 1)
        for k in range(1, groups):
            out = jnp.where(slot == k, pltpu.roll(F[k, core, t], shift + 32 * k, 1), out)
        FM[tile_at(8 * i)] = out

    class Both:
        def __init__(self, src, dst_of, x, y):
            base = sent[0]
            sent[0] += 2
            self.sends, self.receipts = [], []
            for c in (0, 1):
                copy = pltpu.make_async_remote_copy(
                    src_ref=src, dst_ref=dst_of(core),
                    send_sem=ssem.at[base + c], recv_sem=rsem.at[base + core],
                    device_id=(x, y, 2 * z + c), device_id_type=MESH,
                )
                copy.start()
                self.sends.append(copy)
                self.receipts.append(
                    pltpu.make_async_remote_copy(
                        src_ref=src, dst_ref=dst_of(c),
                        send_sem=ssem.at[base + c], recv_sem=rsem.at[base + c],
                        device_id=(x, y, 2 * z + c), device_id_type=MESH,
                    )
                )

        def wait(self):
            for copy in self.receipts:
                copy.wait_recv()
            for copy in self.sends:
                copy.wait_send()

    def columns(rows):
        return lambda c: FR.at[1 - c, rows]

    halos = []

    def collect(q):
        arrived, relays = [], {}
        if q == 0 and nz == 8:
            gather[0][2].wait_recv()
            gather[0][nz - 2].wait_recv()
            step = 2 + (nz - 4) * core
            source, target = lax.rem(z + nz - step, nz), lax.rem(z + step, nz)
            relays[4] = remote(mine(0, source), mine(0, source), (ix, iy, 2 * target + core))
            relays[3] = remote(mine(0, z_back[2]), mine(0, z_back[2]), z_peer[1])
            back = mine(0, z_back[nz - 2])
            relays[nz - 3] = remote(back, back, z_peer[nz - 1])
        for d in (near + list(relays)) if relays else order[::-1]:
            if d in relays:
                relays[d].wait_recv()
            elif not (relays and d in (2, nz - 2)):
                gather[q][d].wait_recv()
            arrived.append(remote(mine(q, z_back[d]), mine(q, z_back[d]), partner))
        dx, here, there, row = ((-1, first, below, p_first), (1, last, above, p_last))[q]
        loop(tiles * q, tiles * (q + 1), pack_field, unroll=4)
        side = pl.ds(part * q, part), pl.ds(PAD + part * q, part)
        out = [Both(FM.at[side[0]], columns(side[1]), ix, toward)]
        out.append(Both(FM.at[here], columns(there), xs[dx], toward))
        out.append(Both(F.at[:, core, row], lambda c: F.at[:, c, there], xs[dx], iy))
        halos.append(out)
        for copy in [forward[q]] + arrived:
            copy.wait_recv()
        return arrived + list(relays.values())

    passed = collect(0)
    loop(2, 8, flows, unroll=2)
    loop(2, 6, advect, unroll=2)
    passed += collect(1)
    loop(8, n_ext - 2, flows, unroll=2)
    loop(6, height // 8 - 2, advect, unroll=2)
    for copy in late:
        copy.wait()
    loop(0, n_ext, build_density, unroll=6)
    for copy in halos[0]:
        copy.wait()
    loop(1, 9, build_field, unroll=4)
    loop(2, 8, strip_flows, unroll=6)
    loop(2, 6, strip_advect, unroll=2)
    for copy in halos[1]:
        copy.wait()

    for flag, ghost, inner in ((at_top, above, PAD), (at_bottom, below, bottom - 1)):
        for h in range(halves):
            for k in range(groups):
                beside = jnp.broadcast_to(F[k, h, inner : inner + 1], (8, LANES))
                F[k, h, ghost] = jnp.where(flag, beside, F[k, h, ghost])
    build_field(0)
    loop(9, n_ext, build_field, unroll=9)
    for flag, ghost, inner in ((at_top, above, PAD), (at_bottom, below, bottom - 1)):
        for side in (0, 1):
            beside = jnp.broadcast_to(Fs[side, inner : inner + 1], (8, LANES))
            Fs[side, ghost] = jnp.where(flag, beside, Fs[side, ghost])
    for i in (0, 1, n_ext - 2, n_ext - 1):
        flows(i)
    for i in (0, 1):
        strip_flows(i)
    loop(8, n_ext, strip_flows, unroll=10)
    for i in (0, 1, height // 8 - 2, height // 8 - 1):
        advect(i)
    loop(0, 2, strip_advect, unroll=2)
    loop(6, height // 8, strip_advect, unroll=2)

    for copy in swap[0] + swap[1] + forward + passed:
        copy.wait_send()
    for q in range(parts):
        for copy in spread[q] + list(gather[q].values()):
            copy.wait_send()


def settle(*refs):
    *ends, sem = refs
    n = len(ends) // 2
    copies = [pltpu.make_async_copy(ends[i], ends[n + i], sem.at[i]) for i in range(n)]
    for copy in copies:
        copy.start()
    for copy in copies:
        copy.wait()


def solution(mesh):
    nx, ny, ng = mesh.shape["gx"], mesh.shape["gy"], mesh.shape["goal"]

    def per_device(potential, cost, obstacle, density, destinations, group_ids):
        goals, height, width = potential.shape
        groups = density.shape[0]
        halves = width // LANES
        rows = height + 2 * PAD
        nz = ng // 2
        f32 = jnp.float32

        def vm(*shape, dtype=f32):
            return pltpu.VMEM(shape, dtype)

        panel = (rows, LANES)
        flat = (height, LANES)
        scratch = [
            vm(goals, halves, *panel), vm(goals, halves, *panel), vm(2, *panel), vm(2, *panel), vm(halves, *panel), vm(2, *panel),
            vm(halves, *flat), vm(halves, *flat, dtype=jnp.int32),
            vm(groups, halves, *panel), vm(2, *panel), vm(*flat), vm(*flat), vm(*panel), vm(*panel),
            vm(groups, halves, *flat), vm(groups, *flat), vm(groups, *flat),
            vm(2, nz, groups, height // (2 * nz), LANES), vm(groups, halves, *panel), vm(2, *panel),
            vm(*flat), vm(2, *panel),
            vm(groups, halves, *panel), vm(groups, halves, *panel), vm(2, *panel), vm(2, *panel),
            vm(groups, halves, *flat),
            pltpu.SMEM((goals,), jnp.int32), pltpu.SMEM((goals,), jnp.int32),
            vm(*flat), vm(*flat), vm(*panel), vm(*panel),
            pltpu.SemaphoreType.DMA((32,)),
            pltpu.SemaphoreType.DMA((88,)),
            pltpu.SemaphoreType.DMA((88,)),
        ]
        anywhere = pl.BlockSpec(memory_space=pltpu.HBM)
        results = pl.pallas_call(
            functools.partial(kernel, nx, ny, nz, goals, groups, height, width),
            out_shape=(
                vm(*potential.shape),
                vm(groups, 2, height, width),
                vm(*density.shape),
            ),
            in_specs=[anywhere] * 6,
            out_specs=(pl.BlockSpec(memory_space=pltpu.VMEM),) * 3,
            scratch_shapes=scratch,
            compiler_params=pltpu.CompilerParams(
                collective_id=0, has_side_effects=True, vmem_limit_bytes=VMEM_LIMIT
            ),
            name="crowd_step",
        )(potential, cost, obstacle, density, destinations, group_ids)
        return pl.pallas_call(
            settle,
            out_shape=tuple(jax.ShapeDtypeStruct(r.shape, f32) for r in results),
            in_specs=[pl.BlockSpec(memory_space=pltpu.VMEM)] * 3,
            out_specs=(pl.BlockSpec(memory_space=pltpu.HBM),) * 3,
            scratch_shapes=[pltpu.SemaphoreType.DMA((3,))],
            compiler_params=pltpu.CompilerParams(vmem_limit_bytes=1 << 20),
            name="settle",
        )(*results)

    in_specs = (
        P("goal", "gx", "gy"),
        P("gx", "gy"),
        P("gx", "gy"),
        P(None, "gx", "gy"),
        P("goal"),
        P("goal"),
    )
    out_specs = (P("goal", "gx", "gy"), P(None, None, "gx", "gy"), P(None, "gx", "gy"))
    return jax.shard_map(
        per_device, mesh=mesh, in_specs=in_specs, out_specs=out_specs, check_vma=False
    )
```
